32 devices in a mesh: row: 4 (over x, core), col: 8 (over z, y).
Axes of the slice: x: 2, y: 2, z: 4, core: 2. Of those that a mesh axis runs over, the one named last changes fastest.
Arguments:
- ground_level_map: float32 [512, 4096], P('row', 'col'), may hold values from 0 to 10
- shoreline_altitude_entries: float32 [32768, 128], P(('row', 'col')), may hold values from 2 to 14
- shoreline_piece_position: int32 [32768], P(('row', 'col')), may hold values from 0 to 511
- lake_panel_locations: float32 [512, 2, 512], P(('row', 'col')), may hold values from 0 to 4096, as said below
- spanned_patch_verticals: int32 [512, 2], P(('row', 'col')), may hold values from 0 to 7, all different within a row; in each aligned block of 16 rows (0 to 15, 16 to 31, ...) at most 6 rows name the same one
Outputs:
- depth: float32 [512, 4096], P('row', 'col')
The draws below stay inside these ranges and needn't reach their ends.
Inputs may be any that keep to these rules, and one draw needn't show every extreme that they name: shoreline_piece_position // 4 numbers a water body of the record's own tile row. `spanned_patch_verticals`: each body names 2 different tile columns; among the 16 bodies of one device no tile column is named more than 6 times, and some device's bodies name some column exactly 6 times. `lake_panel_locations`: entry 0 of a point is a row coordinate inside the rows of the body's tile row, entry 1 a column coordinate of the grid.
All inputs are finite; a program needn't handle non-finite values.
Results may differ from the reference program's by a relative error of at most 0.0003.
Values sent between devices are 32-bit elements; how exact they have to be, the bound alone decides.
No kernel may reach another device: no remote copies, remote signals or barrier semaphores. Data moves between devices by JAX's collectives and lax.ppermute only.
A program may use at most 64 MiB of HBM per device.

```python
import math
import jax
import jax.numpy as jnp
import numpy as np
from jax import lax

PATCH_LINE_TOTAL = 128
PATCH_WIDE_SPAN = 512
EW = 128
SEGS = 4
E_DEV = 1024
NB_DEV = 16
K_COVER = 2
MOST = 6
SWEEPS = 4
P_SIZE = 512
TILE_COLS = 8
NBR = 128
NBODY = 512
EDGES = 32768
MAP_LINE_TOTAL = 512
MAP_WIDE_SPAN = 4096
N_ROW = 4
N_COL = 8


def draw_lake_panel_locations(key, part):
    row_key, centre_key, col_key = jax.random.split(jax.random.fold_in(key, 11), 3)
    band = (jnp.arange(NBODY) // NBR).astype(jnp.float32)
    row_coord = band[:, None] * PATCH_LINE_TOTAL + jax.random.uniform(row_key, (NBODY, P_SIZE), jnp.float32, 0.0, PATCH_LINE_TOTAL)
    window = PATCH_WIDE_SPAN // 2
    centre = jax.random.uniform(centre_key, (NBODY, 1), jnp.float32, 0.0, MAP_WIDE_SPAN - window)
    col_coord = centre + jax.random.uniform(col_key, (NBODY, P_SIZE), jnp.float32, 0.0, window)
    return jnp.stack([row_coord, col_coord], axis=1)


def draw_ground_level_map(key, part):
    phase_key, rough_key = jax.random.split(jax.random.fold_in(key, 23))
    phases = jax.random.uniform(phase_key, (2,), jnp.float32, 0.0, 6.283185307)
    line_pos = jnp.arange(MAP_LINE_TOTAL, dtype=jnp.float32)
    wide_pos = jnp.arange(MAP_WIDE_SPAN, dtype=jnp.float32)
    line_wave = jnp.sin(line_pos * (6.283185307 / (3.7 * PATCH_LINE_TOTAL)) + phases[0])
    wide_wave = jnp.cos(wide_pos * (6.283185307 / (2.3 * PATCH_WIDE_SPAN)) + phases[1])
    smooth_part = line_wave[:, None] * wide_wave[None, :]
    rough_part = jax.random.uniform(rough_key, (MAP_LINE_TOTAL, MAP_WIDE_SPAN), jnp.float32, -1.5, 1.5)
    base_level = 5.0
    return base_level + 2.5 * smooth_part + rough_part


def place_ends(entries, key, least, top_value):
    longest = entries.shape.index(max(entries.shape))
    spots = []
    for shift in (0, 1):
        where = [jax.random.randint(jax.random.fold_in(key, axis), (), 0, length) for axis, length in enumerate(entries.shape)]
        where[longest] = (where[longest] + shift) % entries.shape[longest]
        spots.append(tuple(where))
    return entries.at[spots[0]].set(least).at[spots[1]].set(top_value)


def shard_levels(key, dims, cuts, smallest, top_value):
    factor_of, own = 1.0, jax.random.fold_in(key, 6)
    for axis_at, shards_of in cuts:
        heights = jnp.exp(jax.random.uniform(jax.random.fold_in(own, axis_at), (shards_of,), jnp.float32, smallest / len(cuts), top_value / len(cuts)))
        factor_of = factor_of * jnp.repeat(heights, dims[axis_at] // shards_of).reshape([-1 if axis == axis_at else 1 for axis in range(len(dims))])
    return factor_of


def deal_out(own_key, own, number, rows, amount, top, bound, slope):
    ranking = jax.random.permutation(own_key, amount)
    crowded, ordinary = portions_of(amount, rows * top, bound, slope, True), portions_of(amount, rows * top, bound, slope, False)
    places = jnp.arange(amount)

    def named(lengths, rotation):
        used = int((lengths > 0).sum())
        fixed = max(1, used // 4)
        moved = fixed + (places - fixed + rotation * (used - fixed)) % max(1, amount - fixed)
        return jnp.zeros((amount,), jnp.int32).at[ranking[jnp.where(places < fixed, places, moved)]].set(jnp.asarray(lengths, jnp.int32))

    lengths = jnp.where(number % 4 == 0, named(crowded, number // 4), named(ordinary, number - number // 4 - 1))
    mixed = jax.random.permutation(jax.random.fold_in(own, 3), amount)
    source_of, sink = mixed[0:amount // 2 * 2:2], mixed[1:amount // 2 * 2:2]
    slack = jnp.minimum(lengths[source_of] - 1, bound - lengths[sink]) // 2
    slack = jnp.where((source_of == ranking[0]) | (sink == ranking[0]) | (lengths[sink] == 0), 0, jnp.maximum(slack, 0))
    moved = jax.random.randint(jax.random.fold_in(own, 4), (amount // 2,), 0, 1 << 20) % (slack + 1)
    lengths = lengths.at[source_of].add(-moved).at[sink].add(moved)
    labels = jnp.searchsorted(jnp.cumsum(lengths), jnp.arange(rows * top), side="right").astype(jnp.int32)
    grid = labels.reshape(top, rows).T
    grid = grid[jax.random.permutation(jax.random.fold_in(own, 1), rows)]
    rotation = jax.random.randint(jax.random.fold_in(own, 2), (rows, 1), 0, top)
    return jnp.take_along_axis(grid, (jnp.arange(top)[None, :] + rotation) % top, axis=1)


def portions_of(count, total, bound, lean, full):
    weights = [(1 << 20) // math.isqrt(grade ** lean) + 1 for grade in range(1, count + 1)]
    largest = bound if full else min(bound, max(-(-total // count), total * weights[0] // sum(weights)))
    least = 1 if total - largest >= count - 1 else 0
    given, spare = [largest] + [least] * (count - 1), total - largest - least * (count - 1)
    while spare > 0:
        free = [i for i in range(1, count) if given[i] < largest] or [i for i in range(1, count) if given[i] < bound]
        pool, remaining = sum([weights[i] for i in free]), spare
        for i in free:
            extra = min(bound - given[i], max(1, remaining * weights[i] // pool), spare)
            given[i] = given[i] + extra
            spare = spare - extra
    return np.array(given)


def setup_inputs(seed: int = 0) -> dict:
    key_list = jax.random.split(jax.random.key(seed), 6)
    ground_level_map = draw_ground_level_map(jax.random.fold_in(key_list[5], 71), 0)
    shoreline_altitude_entries = jnp.clip(2.0 + 12.0 * jax.random.uniform(key_list[1], (EDGES, EW), jnp.float32) ** shard_levels(key_list[1], (EDGES, EW), ((0, 32),), -0.2, 0.2), 2.0, 14.0)
    shoreline_piece_position = place_ends(jax.random.randint(key_list[2], (EDGES,), 0, SEGS * NBR), jax.random.fold_in(key_list[2], 1), 0, (SEGS * NBR) - 1).astype(jnp.int32)
    lake_panel_locations = draw_lake_panel_locations(jax.random.fold_in(key_list[5], 71), 0)
    spanned_patch_verticals_keys = jax.random.split(jax.random.fold_in(key_list[4], 1), NBODY // NB_DEV)
    spanned_patch_verticals_turns = jax.random.permutation(jax.random.fold_in(key_list[4], 3), NBODY // NB_DEV)
    spanned_patch_verticals = jax.vmap(lambda own, number: deal_out(jax.random.fold_in(key_list[4], 2), own, number, NB_DEV, TILE_COLS, K_COVER, MOST, 2))(spanned_patch_verticals_keys, spanned_patch_verticals_turns).reshape((NBODY, K_COVER))
    return {"ground_level_map": ground_level_map, "shoreline_altitude_entries": shoreline_altitude_entries, "shoreline_piece_position": shoreline_piece_position, "lake_panel_locations": lake_panel_locations, "spanned_patch_verticals": spanned_patch_verticals}


spread = 4.0
tau_weight = 4.0
flow_gain = 8.0
panel_block = 8


def conduct(depth_ext, ground_altitude, inside):
    center = depth_ext[1:-1, 1:-1]
    height = ground_altitude[1:-1, 1:-1]
    inside_here = inside[1:-1, 1:-1]
    weighted = center
    denominator = jnp.ones_like(center)
    for near_depth, near_height, near_inside in (
        (depth_ext[:-2, 1:-1], ground_altitude[:-2, 1:-1], inside[:-2, 1:-1]),
        (depth_ext[2:, 1:-1], ground_altitude[2:, 1:-1], inside[2:, 1:-1]),
        (depth_ext[1:-1, :-2], ground_altitude[1:-1, :-2], inside[1:-1, :-2]),
        (depth_ext[1:-1, 2:], ground_altitude[1:-1, 2:], inside[1:-1, 2:]),
    ):
        conduct_w = flow_gain * inside_here * near_inside / (1.0 + jnp.abs(height - near_height))
        weighted = weighted + conduct_w * near_depth
        denominator = denominator + conduct_w
    return weighted / denominator


def compact(panels, counts, covers, column):
    covering = jnp.any(covers == column, axis=1).astype(jnp.int32)
    ordering = jnp.argsort(1 - covering, stable=True)
    return panels[ordering], counts[ordering], jnp.sum(covering).astype(jnp.int32)


def tile_water_surface(ordered_entries, ordered_tallies, flooded_tally, pixel_line_offset, vertical_offset, ground_altitude):
    patch_line_total, patch_vertical_total = ground_altitude.shape
    repeat_width = ordered_entries.shape[2] // ordered_tallies.shape[1]
    row_pos = (pixel_line_offset + jnp.arange(patch_line_total, dtype=jnp.int32)).astype(jnp.float32)
    col_pos = (vertical_offset + jnp.arange(patch_vertical_total, dtype=jnp.int32)).astype(jnp.float32)

    def add_block(block_id, accum):
        first_row = (block_id * panel_block).astype(jnp.int32)
        part_panels = lax.dynamic_slice_in_dim(ordered_entries, first_row, panel_block, 0)
        part_counts = lax.dynamic_slice_in_dim(ordered_tallies, first_row, panel_block, 0)
        live_rows = ((first_row + jnp.arange(panel_block, dtype=jnp.int32)) < flooded_tally).astype(jnp.float32)[:, None]
        elev_part = (part_panels[:, 0] * live_rows).reshape(-1)
        count_part = (jnp.repeat(part_counts, repeat_width, axis=1) * live_rows).reshape(-1)
        row_coord = part_panels[:, 1].reshape(-1)
        col_coord = part_panels[:, 2].reshape(-1)
        row_dist = (row_pos[:, None] - row_coord[None, :]) / spread
        col_dist = (col_pos[:, None] - col_coord[None, :]) / spread
        row_kernel = 1.0 / (1.0 + row_dist * row_dist)
        col_kernel = 1.0 / (1.0 + col_dist * col_dist)
        stacked = jnp.concatenate([row_kernel * elev_part[None, :], row_kernel * count_part[None, :]], axis=0)
        return accum + lax.dot_general(stacked, col_kernel, (((1,), (1,)), ((), ())), precision=lax.Precision.HIGHEST, preferred_element_type=jnp.float32)

    blocks = (flooded_tally + panel_block - 1) // panel_block
    accum = lax.fori_loop(0, blocks, add_block, jnp.zeros((2 * patch_line_total, patch_vertical_total), jnp.float32))
    surface = (accum[:patch_line_total] + tau_weight * ground_altitude) / (accum[patch_line_total:] + tau_weight)
    return jnp.maximum(surface - ground_altitude, 0.0)


def reference(ground_level_map, shoreline_altitude_entries, shoreline_piece_position, lake_panel_locations, spanned_patch_verticals):
    bodies_row = NB_DEV * N_COL
    slots_row = SEGS * bodies_row
    row_group = (jnp.arange(EDGES, dtype=jnp.int32) // (E_DEV * N_COL)).astype(jnp.int32)
    segment_ids = shoreline_piece_position + row_group * slots_row
    elev_sums = jax.ops.segment_sum(shoreline_altitude_entries, segment_ids, num_segments=N_ROW * slots_row)
    edge_counts = jax.ops.segment_sum(jnp.ones((EDGES,), jnp.float32), segment_ids, num_segments=N_ROW * slots_row)
    elev_sums = elev_sums.reshape(N_ROW * bodies_row, P_SIZE)
    edge_counts = edge_counts.reshape(N_ROW, bodies_row, SEGS)
    panels = jnp.stack([elev_sums, lake_panel_locations[:, 0], lake_panel_locations[:, 1]], axis=1)
    panels = panels.reshape(N_ROW, bodies_row, 3, P_SIZE)
    covers = spanned_patch_verticals.reshape(N_ROW, bodies_row, K_COVER)

    def one_tile(tile_id):
        pixel_line_number = (tile_id // N_COL).astype(jnp.int32)
        vertical_number = (tile_id % N_COL).astype(jnp.int32)
        ordered_entries, ordered_tallies, flooded_tally = compact(panels[pixel_line_number], edge_counts[pixel_line_number], covers[pixel_line_number], vertical_number)
        ground_altitude = lax.dynamic_slice(ground_level_map, ((pixel_line_number * PATCH_LINE_TOTAL).astype(jnp.int32), (vertical_number * PATCH_WIDE_SPAN).astype(jnp.int32)), (PATCH_LINE_TOTAL, PATCH_WIDE_SPAN))
        return tile_water_surface(ordered_entries, ordered_tallies, flooded_tally, pixel_line_number * PATCH_LINE_TOTAL, vertical_number * PATCH_WIDE_SPAN, ground_altitude)

    tile_depths = lax.map(one_tile, jnp.arange(N_ROW * N_COL, dtype=jnp.int32))
    depth = tile_depths.reshape(N_ROW, N_COL, PATCH_LINE_TOTAL, PATCH_WIDE_SPAN).transpose(0, 2, 1, 3).reshape(MAP_LINE_TOTAL, MAP_WIDE_SPAN)
    inside = jnp.pad(jnp.ones((MAP_LINE_TOTAL, MAP_WIDE_SPAN), jnp.float32), 1)
    ground_altitude = jnp.pad(ground_level_map, 1)
    for sweep_index in range(SWEEPS):
        depth = conduct(jnp.pad(depth, 1), ground_altitude, inside)
    return depth
```

```python
import functools

import jax
import jax.numpy as jnp
from jax import lax
from jax.experimental import pallas as pl
from jax.experimental.pallas import tpu as pltpu
from jax.sharding import PartitionSpec as P

SEGS = 4
SWEEPS = 4
MOST = 6
LANES = 128

spread = 4.0
tau_weight = 4.0
flow_gain = 8.0

F32 = jnp.float32
BF16 = jnp.bfloat16
VMEM_LIMIT = 48 * 1024 * 1024


def vmem():
    return pl.BlockSpec(memory_space=pltpu.VMEM)


def smem():
    return pl.BlockSpec(memory_space=pltpu.SMEM)


def params():
    return pltpu.CompilerParams(vmem_limit_bytes=VMEM_LIMIT)


def one_hot(cond):
    return jnp.where(cond, 1.0, 0.0).astype(BF16)


def segment_kernel(ids_ref, entry_ref, out_ref):
    owners, rows, _ = out_ref.shape
    bodies = rows // (SEGS + 1)
    chunks = ids_ref.shape[0]
    seg_iota = lax.broadcasted_iota(jnp.int32, (owners * bodies * SEGS, LANES), 0)
    body_iota = lax.broadcasted_iota(jnp.int32, (owners * bodies, LANES), 0)
    lane_seg = lax.broadcasted_iota(jnp.int32, (LANES, LANES), 0) // (LANES // SEGS)
    ids = [ids_ref[k : k + 1, :] for k in range(chunks)]
    by_segment = jnp.concatenate([one_hot(seg_iota == v) for v in ids], axis=1)
    by_body = jnp.concatenate([one_hot(body_iota == v // SEGS) for v in ids], axis=1)
    by_lane = jnp.concatenate([one_hot(lane_seg == v % SEGS) for v in ids], axis=1)
    entries = entry_ref[...]
    high = entries.astype(BF16)
    low = (entries - high.astype(F32)).astype(BF16)
    both = jnp.dot(
        by_segment, jnp.concatenate([high, low], axis=1), preferred_element_type=F32
    )
    sums = both[:, :LANES] + both[:, LANES:]
    counts = lax.dot_general(
        by_body, by_lane, (((1,), (1,)), ((), ())), preferred_element_type=F32
    )
    for owner in range(owners):
        step = bodies * SEGS
        out_ref[owner, :step, :] = sums[owner * step : (owner + 1) * step]
        out_ref[owner, step:, :] = counts[owner * bodies : (owner + 1) * bodies]


def locations_kernel(cover_ref, place_ref, out_ref, used_ref):
    columns = out_ref.shape[0]
    bodies, covers = cover_ref.shape
    out_ref[...] = jnp.zeros_like(out_ref)
    for column in range(columns):
        used_ref[column] = 0
    for body_id in range(bodies):
        rows = place_ref[body_id]
        tile = jnp.concatenate(
            [
                rows[axis : axis + 1, s * LANES : (s + 1) * LANES]
                for axis in range(2)
                for s in range(SEGS)
            ],
            axis=0,
        )
        for k in range(covers):
            column = cover_ref[body_id, k]
            slot = used_ref[column]
            used_ref[column] = slot + 1
            out_ref[column, slot] = tile


def owner_kernel(cover_ref, part_ref, out_ref, total_ref, used_ref):
    columns = out_ref.shape[0]
    bodies, covers = cover_ref.shape
    total = part_ref[0]
    for source in range(1, part_ref.shape[0]):
        total = total + part_ref[source]
    total_ref[...] = total
    out_ref[...] = jnp.zeros_like(out_ref)
    for column in range(columns):
        used_ref[column] = 0
    for body_id in range(bodies):
        sums = total_ref[body_id * SEGS : (body_id + 1) * SEGS, :]
        count = total_ref[bodies * SEGS + body_id : bodies * SEGS + body_id + 1, :]
        for k in range(covers):
            column = cover_ref[body_id, k]
            slot = used_ref[column]
            used_ref[column] = slot + 1
            out_ref[column, pl.ds(slot * SEGS, SEGS), :] = sums
            out_ref[column, pl.ds(MOST * SEGS + slot, 1), :] = count


def lorentz(size, origin, coord):
    shifted = (coord - origin) * (1.0 / spread)
    index = lax.broadcasted_iota(jnp.int32, (size, LANES), 0).astype(F32) * (1.0 / spread)
    distance = index - shifted
    return 1.0 / (1.0 + distance * distance)


def column_kernel(place_ref, out_ref):
    tile_columns = out_ref.shape[1]
    origin = (lax.axis_index("col") * tile_columns).astype(F32)

    @pl.loop(0, MOST)
    def _(slot):
        tile = place_ref[0, slot]
        for s in range(SEGS):
            value = lorentz(tile_columns, origin, tile[SEGS + s : SEGS + s + 1, :])
            out_ref[0, :, pl.ds(pl.multiple_of((slot * SEGS + s) * LANES, LANES), LANES)] = (
                value.astype(BF16)
            )


def surface_kernel(place_ref, sums_ref, column_ref, ground_ref, depth_ref, strip_ref, acc_ref, mean_ref):
    owner = pl.program_id(0)
    tile_rows, _ = ground_ref.shape
    origin = (lax.axis_index("row") * tile_rows).astype(F32)

    @pl.when(owner == 0)
    def _():
        acc_ref[...] = jnp.zeros_like(acc_ref)
        elev = jnp.sum(sums_ref[:, : MOST * SEGS, :], axis=0)
        count = jnp.sum(sums_ref[:, MOST * SEGS : MOST * SEGS + 8, :], axis=0)
        elev = jnp.sum(jnp.sum(elev, axis=0, keepdims=True), axis=1, keepdims=True)
        count = jnp.sum(jnp.sum(count, axis=0, keepdims=True), axis=1, keepdims=True)
        mean_ref[...] = jnp.broadcast_to(elev / jnp.maximum(count * SEGS, 1.0), mean_ref.shape)

    mean = mean_ref[0:1, :]
    for slot in range(MOST):
        tile = place_ref[0, slot]
        elev_parts, count_parts = [], []
        for s in range(SEGS):
            count = sums_ref[owner, MOST * SEGS + slot : MOST * SEGS + slot + 1, :]
            lane = s * (LANES // SEGS)
            count = jnp.broadcast_to(count[:, lane : lane + 1], (1, LANES))
            elev = sums_ref[owner, slot * SEGS + s : slot * SEGS + s + 1, :] - mean * count
            value = lorentz(tile_rows, origin, tile[s : s + 1, :])
            elev_parts.append((value * elev).astype(BF16))
            count_parts.append((value * count).astype(BF16))
        stacked = jnp.concatenate(
            [jnp.concatenate(elev_parts, axis=1), jnp.concatenate(count_parts, axis=1)], axis=0
        )
        points = SEGS * LANES
        acc_ref[...] += lax.dot_general(
            stacked,
            column_ref[0, :, slot * points : (slot + 1) * points],
            (((1,), (1,)), ((), ())),
            preferred_element_type=F32,
        )

    @pl.when(owner == pl.num_programs(0) - 1)
    def _():
        ground = ground_ref[...]
        den = acc_ref[tile_rows:, :]
        base = jnp.broadcast_to(mean_ref[0:1, 0:1], ground.shape)
        depth = (acc_ref[:tile_rows, :] + (base - ground) * den) / (den + tau_weight)
        depth = jnp.maximum(depth, 0.0)
        depth_ref[...] = depth
        strip_ref[...] = jnp.concatenate(
            [
                depth[:SWEEPS],
                depth[tile_rows - SWEEPS :],
                ground[:SWEEPS],
                ground[tile_rows - SWEEPS :],
            ],
            axis=0,
        )


def neighbour_rows(strip_ref, row_count):
    me = lax.axis_index("row")
    block = 4 * SWEEPS
    above = pl.multiple_of(jnp.maximum(me - 1, 0) * block, block)
    below = pl.multiple_of(jnp.minimum(me + 1, row_count - 1) * block, block)
    above = strip_ref[pl.ds(above, block), :]
    below = strip_ref[pl.ds(below, block), :]
    return (
        above[SWEEPS : 2 * SWEEPS],
        below[:SWEEPS],
        above[3 * SWEEPS :],
        below[2 * SWEEPS : 3 * SWEEPS],
    )


def edge_kernel(row_count, strip_ref, depth_ref, ground_ref, left_ref, right_ref):
    tile_rows, tile_columns = depth_ref.shape
    depth_up, depth_down, ground_up, ground_down = neighbour_rows(strip_ref, row_count)
    for out_ref, start, pick in (
        (left_ref, 0, 0),
        (right_ref, tile_columns - LANES, LANES - SWEEPS),
    ):
        lanes = slice(start, start + LANES)
        for k, (ref, up, down) in enumerate(
            ((depth_ref, depth_up, depth_down), (ground_ref, ground_up, ground_down))
        ):
            main = jnp.transpose(ref[:, lanes])[pick : pick + SWEEPS]
            outer = jnp.concatenate([up[:, lanes], down[:, lanes]], axis=0)
            outer = jnp.transpose(outer)[pick : pick + SWEEPS]
            out_ref[k * SWEEPS : (k + 1) * SWEEPS, :tile_rows] = main
            out_ref[k * SWEEPS : (k + 1) * SWEEPS, tile_rows:] = jnp.concatenate(
                [outer, jnp.zeros((SWEEPS, LANES - 2 * SWEEPS), F32)], axis=1
            )


def sweep_kernel(
    row_count, col_count, strip_ref, left_ref, right_ref, depth_ref, ground_ref, out_ref, height_ref, land_ref
):
    tile_rows, tile_columns = depth_ref.shape
    pad_rows, pad_cols = 8, LANES
    rows, cols = height_ref.shape
    depth_up, depth_down, ground_up, ground_down = neighbour_rows(strip_ref, row_count)
    for ref, inner_ref, up, down, k in (
        (height_ref, depth_ref, depth_up, depth_down, 0),
        (land_ref, ground_ref, ground_up, ground_down, SWEEPS),
    ):
        ref[...] = jnp.zeros_like(ref)
        inner = slice(pad_cols, pad_cols + tile_columns)
        ref[pad_rows : pad_rows + tile_rows, inner] = inner_ref[...]
        ref[pad_rows - SWEEPS : pad_rows, inner] = up
        ref[pad_rows + tile_rows : pad_rows + tile_rows + SWEEPS, inner] = down
        for side_ref, first in (
            (left_ref, pad_cols - SWEEPS),
            (right_ref, pad_cols + tile_columns),
        ):
            main = jnp.transpose(side_ref[:, :tile_rows])[:, k : k + SWEEPS]
            outer = jnp.transpose(side_ref[:, tile_rows:])[: 2 * SWEEPS, k : k + SWEEPS]
            lanes = slice(first, first + SWEEPS)
            ref[pad_rows : pad_rows + tile_rows, lanes] = main
            ref[pad_rows - SWEEPS : pad_rows, lanes] = outer[:SWEEPS]
            ref[pad_rows + tile_rows : pad_rows + tile_rows + SWEEPS, lanes] = outer[SWEEPS:]

    row_id = lax.broadcasted_iota(jnp.int32, (rows, cols), 0) + (
        lax.axis_index("row") * tile_rows - pad_rows
    )
    col_id = lax.broadcasted_iota(jnp.int32, (rows, cols), 1) + (
        lax.axis_index("col") * tile_columns - pad_cols
    )
    grid_rows, grid_cols = tile_rows * row_count, tile_columns * col_count
    land = land_ref[...]
    down = flow_gain / (1.0 + jnp.abs(land - pltpu.roll(land, rows - 1, 0)))
    right = flow_gain / (1.0 + jnp.abs(land - pltpu.roll(land, cols - 1, 1)))
    down = jnp.where((row_id >= 0) & (row_id < grid_rows - 1), down, 0.0)
    right = jnp.where((col_id >= 0) & (col_id < grid_cols - 1), right, 0.0)
    up = pltpu.roll(down, 1, 0)
    left = pltpu.roll(right, 1, 1)
    scale = 1.0 / (1.0 + up + down + left + right)
    up, down, left, right = up * scale, down * scale, left * scale, right * scale
    height = height_ref[...]
    for _ in range(SWEEPS):
        height = (
            height * scale
            + up * pltpu.roll(height, 1, 0)
            + down * pltpu.roll(height, rows - 1, 0)
            + left * pltpu.roll(height, 1, 1)
            + right * pltpu.roll(height, cols - 1, 1)
        )
    out_ref[...] = height[pad_rows : pad_rows + tile_rows, pad_cols : pad_cols + tile_columns]


def shift(values, axis, step):
    count = lax.axis_size(axis)
    return lax.ppermute(values, axis, [(i, (i + step) % count) for i in range(count)])


def body(
    ground_level_map,
    shoreline_altitude_entries,
    shoreline_piece_position,
    lake_panel_locations,
    spanned_patch_verticals,
):
    tile_rows, tile_columns = ground_level_map.shape
    col_count = lax.axis_size("col")
    row_count = lax.axis_size("row")
    records, _ = shoreline_altitude_entries.shape
    bodies, _ = spanned_patch_verticals.shape
    covers = spanned_patch_verticals
    points = SEGS * LANES

    places = pl.pallas_call(
        locations_kernel,
        out_shape=jax.ShapeDtypeStruct((col_count, MOST, 2 * SEGS, LANES), F32),
        in_specs=[smem(), vmem()],
        out_specs=vmem(),
        scratch_shapes=[pltpu.SMEM((col_count,), jnp.int32)],
        compiler_params=params(),
    )(covers, lake_panel_locations)
    places = lax.all_to_all(places, "col", 0, 0, tiled=True)

    parts = pl.pallas_call(
        segment_kernel,
        out_shape=jax.ShapeDtypeStruct((col_count, bodies * (SEGS + 1), LANES), F32),
        in_specs=[vmem(), vmem()],
        out_specs=vmem(),
        compiler_params=params(),
    )(shoreline_piece_position.reshape(records // LANES, LANES), shoreline_altitude_entries)
    parts = lax.all_to_all(parts, "col", 0, 0, tiled=True)

    column_kernels = pl.pallas_call(
        column_kernel,
        grid=(col_count,),
        out_shape=jax.ShapeDtypeStruct((col_count, tile_columns, MOST * points), BF16),
        in_specs=[pl.BlockSpec((1, MOST, 2 * SEGS, LANES), lambda o: (o, 0, 0, 0))],
        out_specs=pl.BlockSpec((1, tile_columns, MOST * points), lambda o: (o, 0, 0)),
        compiler_params=params(),
        cost_estimate=pl.CostEstimate(
            flops=8 * col_count * tile_columns * MOST * points,
            transcendentals=0,
            bytes_accessed=2 * col_count * tile_columns * MOST * points,
        ),
    )(places)

    slot_rows = MOST * SEGS + 8
    sums = pl.pallas_call(
        owner_kernel,
        out_shape=jax.ShapeDtypeStruct((col_count, slot_rows, LANES), F32),
        in_specs=[smem(), vmem()],
        out_specs=vmem(),
        scratch_shapes=[
            pltpu.VMEM((bodies * (SEGS + 1), LANES), F32),
            pltpu.SMEM((col_count,), jnp.int32),
        ],
        compiler_params=params(),
    )(covers, parts)
    sums = lax.all_to_all(sums, "col", 0, 0, tiled=True)

    depth, strips = pl.pallas_call(
        surface_kernel,
        grid=(col_count,),
        out_shape=(
            jax.ShapeDtypeStruct((tile_rows, tile_columns), F32),
            jax.ShapeDtypeStruct((4 * SWEEPS, tile_columns), F32),
        ),
        in_specs=[
            pl.BlockSpec((1, MOST, 2 * SEGS, LANES), lambda o: (o, 0, 0, 0)),
            pl.BlockSpec((col_count, slot_rows, LANES), lambda o: (0, 0, 0)),
            pl.BlockSpec((1, tile_columns, MOST * points), lambda o: (o, 0, 0)),
            pl.BlockSpec((tile_rows, tile_columns), lambda o: (0, 0)),
        ],
        out_specs=(
            pl.BlockSpec((tile_rows, tile_columns), lambda o: (0, 0)),
            pl.BlockSpec((4 * SWEEPS, tile_columns), lambda o: (0, 0)),
        ),
        scratch_shapes=[
            pltpu.VMEM((2 * tile_rows, tile_columns), F32),
            pltpu.VMEM((8, LANES), F32),
        ],
        compiler_params=params(),
    )(places, sums, column_kernels, ground_level_map)

    strips = lax.all_gather(strips, "row", axis=0, tiled=True)
    edge_shape = jax.ShapeDtypeStruct((2 * SWEEPS, tile_rows + LANES), F32)
    left, right = pl.pallas_call(
        functools.partial(edge_kernel, row_count),
        out_shape=(edge_shape, edge_shape),
        in_specs=[vmem()] * 3,
        out_specs=(vmem(), vmem()),
        compiler_params=params(),
    )(strips, depth, ground_level_map)
    from_left = shift(right, "col", 1)
    from_right = shift(left, "col", -1)

    scratch = pltpu.VMEM((tile_rows + 16, tile_columns + 2 * LANES), F32)
    return pl.pallas_call(
        functools.partial(sweep_kernel, row_count, col_count),
        out_shape=jax.ShapeDtypeStruct((tile_rows, tile_columns), F32),
        in_specs=[vmem()] * 5,
        out_specs=vmem(),
        scratch_shapes=[scratch, scratch],
        compiler_params=params(),
    )(strips, from_left, from_right, depth, ground_level_map)


def solution(mesh):
    in_specs = (
        P("row", "col"),
        P(("row", "col"), None),
        P(("row", "col")),
        P(("row", "col"), None, None),
        P(("row", "col"), None),
    )
    out_specs = P("row", "col")
    return jax.shard_map(body, mesh=mesh, in_specs=in_specs, out_specs=out_specs, check_vma=False)
```

```python
import functools

import jax
import jax.numpy as jnp
from jax import lax
from jax.experimental import pallas as pl
from jax.experimental.pallas import tpu as pltpu
from jax.sharding import PartitionSpec as P

SEGS = 4
SWEEPS = 4
MOST = 6
LANES = 128

spread = 4.0
tau_weight = 4.0
flow_gain = 8.0

F32 = jnp.float32
BF16 = jnp.bfloat16
VMEM_LIMIT = 24 * 1024 * 1024


def vmem():
    return pl.BlockSpec(memory_space=pltpu.VMEM)


def smem():
    return pl.BlockSpec(memory_space=pltpu.SMEM)


def params(limit=VMEM_LIMIT):
    return pltpu.CompilerParams(vmem_limit_bytes=limit)


def one_hot(cond):
    return jnp.where(cond, 1.0, 0.0).astype(BF16)


def pack_kernel(cover_ref, ids_hbm, entry_hbm, place_hbm, out_ref, ids_ref, entry_ref, place_ref, used_ref, sems):
    owners, _, _ = out_ref.shape
    covers, bodies = cover_ref.shape
    copies = [
        pltpu.make_async_copy(source, target, sems.at[k])
        for k, (source, target) in enumerate(
            ((ids_hbm, ids_ref), (entry_hbm, entry_ref), (place_hbm, place_ref))
        )
    ]
    for copy in copies:
        copy.start()
    chunks = ids_ref.shape[0]
    sum_rows, count_rows = bodies * SEGS, bodies // 2
    first_slot = sum_rows + count_rows
    out_ref[:, first_slot:, :] = jnp.zeros((owners, MOST * 8, LANES), F32)
    copies[0].wait()
    seg_iota = lax.broadcasted_iota(jnp.int32, (owners * sum_rows, LANES), 0)
    pair_iota = lax.broadcasted_iota(jnp.int32, (owners * count_rows, LANES), 0)
    lane_group = lax.broadcasted_iota(jnp.int32, (LANES, LANES), 0) // 16
    ids = [ids_ref[k : k + 1, :] for k in range(chunks)]
    by_pair = jnp.concatenate([one_hot(pair_iota == v // 8) for v in ids], axis=1)
    by_lane = jnp.concatenate([one_hot(lane_group == v % 8) for v in ids], axis=1)
    counts = lax.dot_general(
        by_pair, by_lane, (((1,), (1,)), ((), ())), preferred_element_type=F32
    )
    by_segment = jnp.concatenate([one_hot(seg_iota == v) for v in ids], axis=1)
    copies[1].wait()
    entries = entry_ref[...]
    high = entries.astype(BF16)
    low = (entries - high.astype(F32)).astype(BF16)
    both = jnp.dot(
        by_segment, jnp.concatenate([high, low], axis=1), preferred_element_type=F32
    )
    sums = both[:, :LANES] + both[:, LANES:]
    for owner in range(owners):
        out_ref[owner, :sum_rows, :] = sums[owner * sum_rows : (owner + 1) * sum_rows]
        out_ref[owner, sum_rows:first_slot, :] = counts[
            owner * count_rows : (owner + 1) * count_rows
        ]
    copies[2].wait()
    for column in range(owners):
        used_ref[column] = 0
    for body_id in range(bodies):
        rows = place_ref[body_id]
        tile = jnp.concatenate(
            [
                rows[axis : axis + 1, s * LANES : (s + 1) * LANES]
                for axis in range(2)
                for s in range(SEGS)
            ],
            axis=0,
        )
        for k in range(covers):
            column = cover_ref[k, body_id]
            slot = used_ref[column]
            used_ref[column] = slot + 1
            out_ref[column, pl.ds(pl.multiple_of(first_slot + slot * 8, 8), 8), :] = tile


def owner_kernel(cover_ref, part_ref, out_ref, total_ref, used_ref):
    columns = out_ref.shape[0]
    covers, bodies = cover_ref.shape
    rows = total_ref.shape[0]
    total = part_ref[0, :rows, :]
    for source in range(1, part_ref.shape[0]):
        total = total + part_ref[source, :rows, :]
    total_ref[...] = total
    out_ref[...] = jnp.zeros_like(out_ref)
    for column in range(columns):
        used_ref[column] = 0
    for body_id in range(bodies):
        sums = total_ref[body_id * SEGS : (body_id + 1) * SEGS, :]
        row, lane = bodies * SEGS + body_id // 2, 64 * (body_id % 2)
        count = total_ref[row : row + 1, lane : lane + 64]
        for k in range(covers):
            column = cover_ref[k, body_id]
            slot = used_ref[column]
            used_ref[column] = slot + 1
            out_ref[column, pl.ds(slot * SEGS, SEGS), :] = sums
            out_ref[column, pl.ds(MOST * SEGS + slot, 1), :64] = count


def lorentz(base, step):
    distance = base + step
    return 1.0 / (1.0 + distance * distance)


def cell_base(origin, coord):
    index = lax.broadcasted_iota(jnp.int32, (16, LANES), 0).astype(F32) * (1.0 / spread)
    return index - (coord - origin) * (1.0 / spread)


def column_block(place_ref, owner, row, origin, starts):
    parts = []
    for s in range(SEGS):
        base = cell_base(origin, place_ref[owner, row + SEGS + s : row + SEGS + s + 1, :])
        parts.append(
            jnp.concatenate(
                [
                    lorentz(base, (start + j) / spread).astype(BF16)
                    for start in starts
                    for j in range(0, LANES, 16)
                ],
                axis=0,
            )
        )
    return jnp.concatenate(parts, axis=1)


def times_stack(columns, stack):
    return lax.dot_general(
        columns, stack, (((1,), (1,)), ((), ())), preferred_element_type=F32
    )


def surface(acc, mean, ground):
    tile_rows = ground.shape[0]
    num = jnp.transpose(acc[:, :tile_rows])
    den = jnp.transpose(acc[:, tile_rows:])
    depth = (num + (mean - ground) * den) / (den + tau_weight)
    return jnp.maximum(depth, 0.0)


def outer_kernel(
    first_slot, place_ref, sums_ref, ground_ref, depth_ref, left_ref, right_ref, stack_ref, mean_ref, acc_ref
):
    tile_rows, tile_columns = ground_ref.shape
    owners = sums_ref.shape[0]
    row_origin = (lax.axis_index("row") * tile_rows).astype(F32)
    col_origin = (lax.axis_index("col") * tile_columns).astype(F32)
    elev = jnp.sum(sums_ref[:, : MOST * SEGS, :], axis=0)
    count = jnp.sum(sums_ref[:, MOST * SEGS : MOST * SEGS + 8, :], axis=0)
    elev = jnp.sum(jnp.sum(elev, axis=0, keepdims=True), axis=1, keepdims=True)
    count = jnp.sum(jnp.sum(count, axis=0, keepdims=True), axis=1, keepdims=True)
    mean = elev / jnp.maximum(count * (LANES / 16), 1.0)
    mean_ref[...] = jnp.broadcast_to(mean, mean_ref.shape)
    acc_ref[...] = jnp.zeros_like(acc_ref)
    starts = (0, tile_columns - LANES)

    @pl.loop(0, owners)
    def _(owner):
        for slot in range(MOST):
            row = first_slot + slot * 8
            blocks = []
            for s in range(SEGS):
                here = sums_ref[owner, MOST * SEGS + slot : MOST * SEGS + slot + 1, s * 16 : s * 16 + 1]
                part = sums_ref[owner, slot * SEGS + s : slot * SEGS + s + 1, :] - mean * here
                weight = jnp.broadcast_to(here, (16, LANES))
                part = jnp.broadcast_to(part, (16, LANES))
                base = cell_base(row_origin, place_ref[owner, row + s : row + s + 1, :])
                values = [lorentz(base, i / spread) for i in range(0, tile_rows, 16)]
                block = jnp.concatenate(
                    [(v * part).astype(BF16) for v in values]
                    + [(v * weight).astype(BF16) for v in values],
                    axis=0,
                )
                stack_ref[owner * (MOST * SEGS) + slot * SEGS + s] = block
                blocks.append(block)
            columns = column_block(place_ref, owner, row, col_origin, starts)
            acc_ref[...] += times_stack(columns, jnp.concatenate(blocks, axis=1))

    ground = jnp.concatenate(
        [ground_ref[:, start : start + LANES] for start in starts], axis=1
    )
    depth = surface(acc_ref[...], mean, ground)
    depth_ref[...] = depth
    for out_ref, start, pick in ((left_ref, 0, 0), (right_ref, LANES, LANES - SWEEPS)):
        for k, values in enumerate((depth, ground)):
            out_ref[k * SWEEPS : (k + 1) * SWEEPS, :] = jnp.transpose(
                values[:, start : start + LANES]
            )[pick : pick + SWEEPS]


def inner_kernel(first_slot, place_ref, stack_ref, mean_ref, ground_ref, depth_ref, acc_ref):
    tile_columns = ground_ref.shape[1]
    owners = place_ref.shape[0]
    col_origin = (lax.axis_index("col") * tile_columns).astype(F32)
    acc_ref[...] = jnp.zeros_like(acc_ref)
    starts = tuple(range(LANES, tile_columns - LANES, LANES))

    @pl.loop(0, owners)
    def _(owner):
        for slot in range(MOST):
            columns = column_block(place_ref, owner, first_slot + slot * 8, col_origin, starts)
            stack = jnp.concatenate(
                [stack_ref[owner * (MOST * SEGS) + slot * SEGS + s] for s in range(SEGS)], axis=1
            )
            acc_ref[...] += times_stack(columns, stack)

    ground = ground_ref[:, LANES : tile_columns - LANES]
    depth_ref[...] = surface(acc_ref[...], mean_ref[0:1, 0:1], ground)


def paste(outer, inner):
    return jnp.concatenate([outer[:, :LANES], inner, outer[:, LANES:]], axis=1)


def strip_kernel(outer_ref, inner_ref, ground_ref, left_ref, right_ref, strip_ref):
    tile_rows, tile_columns = ground_ref.shape
    sides = jnp.concatenate(
        [left_ref[:SWEEPS], right_ref[:SWEEPS], left_ref[SWEEPS:], right_ref[SWEEPS:]], axis=0
    )
    sides = jnp.transpose(sides)
    row = 0
    for k in range(2):
        for first in (0, tile_rows - SWEEPS):
            rows = slice(first, first + SWEEPS)
            if k == 0:
                main = paste(outer_ref[rows, :], inner_ref[rows, :])
            else:
                main = ground_ref[rows, :]
            strip_ref[row : row + SWEEPS, :tile_columns] = main
            strip_ref[row : row + SWEEPS, tile_columns:] = jnp.concatenate(
                [
                    sides[rows, 2 * SWEEPS * k : 2 * SWEEPS * (k + 1)],
                    jnp.zeros((SWEEPS, LANES - 2 * SWEEPS), F32),
                ],
                axis=1,
            )
            row += SWEEPS


def neighbour_rows(strip_ref, row_count):
    me = lax.axis_index("row")
    block = 4 * SWEEPS
    above = pl.multiple_of(jnp.maximum(me - 1, 0) * block, block)
    below = pl.multiple_of(jnp.minimum(me + 1, row_count - 1) * block, block)
    above = strip_ref[pl.ds(above, block), :]
    below = strip_ref[pl.ds(below, block), :]
    return (
        above[SWEEPS : 2 * SWEEPS],
        below[:SWEEPS],
        above[3 * SWEEPS :],
        below[2 * SWEEPS : 3 * SWEEPS],
    )


def sweep_kernel(
    row_count,
    col_count,
    strip_ref,
    left_ref,
    right_ref,
    outer_ref,
    inner_ref,
    ground_ref,
    out_ref,
    height_ref,
    land_ref,
):
    tile_rows, tile_columns = ground_ref.shape
    pad_rows, pad_cols = 8, LANES
    rows, cols = height_ref.shape
    depth_up, depth_down, ground_up, ground_down = neighbour_rows(strip_ref, row_count)
    sides = jnp.transpose(jnp.concatenate([left_ref[...], right_ref[...]], axis=0))
    last = pad_rows + tile_rows
    for ref, up, down, k in (
        (height_ref, depth_up, depth_down, 0),
        (land_ref, ground_up, ground_down, SWEEPS),
    ):
        ref[:pad_rows, :] = jnp.zeros((pad_rows, cols), F32)
        ref[last:, :] = jnp.zeros((rows - last, cols), F32)
        inner = slice(pad_cols, pad_cols + tile_columns)
        if k == 0:
            ref[pad_rows:last, pad_cols : 2 * pad_cols] = outer_ref[:, :LANES]
            ref[pad_rows:last, 2 * pad_cols : cols - 2 * pad_cols] = inner_ref[...]
            ref[pad_rows:last, cols - 2 * pad_cols : cols - pad_cols] = outer_ref[:, LANES:]
        else:
            ref[pad_rows:last, inner] = ground_ref[...]
        ref[pad_rows - SWEEPS : pad_rows, inner] = up[:, :tile_columns]
        ref[last : last + SWEEPS, inner] = down[:, :tile_columns]
        blank = jnp.zeros((tile_rows, LANES - SWEEPS), F32)
        left = sides[:, k : k + SWEEPS]
        right = sides[:, 2 * SWEEPS + k : 3 * SWEEPS + k]
        ref[pad_rows:last, :pad_cols] = jnp.concatenate([blank, left], axis=1)
        ref[pad_rows:last, cols - pad_cols :] = jnp.concatenate([right, blank], axis=1)
        for first, corner in ((pad_rows - SWEEPS, up), (last, down)):
            corner = corner[:, tile_columns : tile_columns + 2 * SWEEPS]
            ref[first : first + SWEEPS, pad_cols - SWEEPS : pad_cols] = corner[:, :SWEEPS]
            ref[first : first + SWEEPS, cols - pad_cols : cols - pad_cols + SWEEPS] = corner[:, SWEEPS:]

    row_id = lax.broadcasted_iota(jnp.int32, (rows, cols), 0) + (
        lax.axis_index("row") * tile_rows - pad_rows
    )
    col_id = lax.broadcasted_iota(jnp.int32, (rows, cols), 1) + (
        lax.axis_index("col") * tile_columns - pad_cols
    )
    grid_rows, grid_cols = tile_rows * row_count, tile_columns * col_count
    land = land_ref[...]
    down = flow_gain / (1.0 + jnp.abs(land - pltpu.roll(land, rows - 1, 0)))
    right = flow_gain / (1.0 + jnp.abs(land - pltpu.roll(land, cols - 1, 1)))
    down = jnp.where((row_id >= 0) & (row_id < grid_rows - 1), down, 0.0)
    right = jnp.where((col_id >= 0) & (col_id < grid_cols - 1), right, 0.0)
    up = pltpu.roll(down, 1, 0)
    left = pltpu.roll(right, 1, 1)
    scale = 1.0 / (1.0 + up + down + left + right)
    up, down, left, right = up * scale, down * scale, left * scale, right * scale
    height = height_ref[...]
    for _ in range(SWEEPS):
        height = (
            height * scale
            + up * pltpu.roll(height, 1, 0)
            + down * pltpu.roll(height, rows - 1, 0)
            + left * pltpu.roll(height, 1, 1)
            + right * pltpu.roll(height, cols - 1, 1)
        )
    out_ref[...] = height[pad_rows : pad_rows + tile_rows, pad_cols : pad_cols + tile_columns]


def shift(values, axis, step):
    count = lax.axis_size(axis)
    return lax.ppermute(values, axis, [(i, (i + step) % count) for i in range(count)])


def body(
    ground_level_map,
    shoreline_altitude_entries,
    shoreline_piece_position,
    lake_panel_locations,
    spanned_patch_verticals,
):
    tile_rows, tile_columns = ground_level_map.shape
    col_count = lax.axis_size("col")
    row_count = lax.axis_size("row")
    records, _ = shoreline_altitude_entries.shape
    bodies, _ = spanned_patch_verticals.shape
    covers = spanned_patch_verticals.T
    first_slot = bodies * SEGS + bodies // 2
    hbm = pl.BlockSpec(memory_space=pltpu.HBM)

    parts = pl.pallas_call(
        pack_kernel,
        out_shape=jax.ShapeDtypeStruct((col_count, first_slot + MOST * 8, LANES), F32),
        in_specs=[smem(), hbm, hbm, hbm],
        out_specs=vmem(),
        scratch_shapes=[
            pltpu.VMEM((records // LANES, LANES), jnp.int32),
            pltpu.VMEM((records, LANES), F32),
            pltpu.VMEM(lake_panel_locations.shape, F32),
            pltpu.SMEM((col_count,), jnp.int32),
            pltpu.SemaphoreType.DMA((3,)),
        ],
        compiler_params=params(60 * 1024 * 1024),
    )(
        covers,
        shoreline_piece_position.reshape(records // LANES, LANES),
        shoreline_altitude_entries,
        lake_panel_locations,
    )
    parts = lax.all_to_all(parts, "col", 0, 0, tiled=True)

    slot_rows = MOST * SEGS + 8
    sums = pl.pallas_call(
        owner_kernel,
        out_shape=jax.ShapeDtypeStruct((col_count, slot_rows, LANES), F32),
        in_specs=[smem(), vmem()],
        out_specs=vmem(),
        scratch_shapes=[
            pltpu.VMEM((first_slot, LANES), F32),
            pltpu.SMEM((col_count,), jnp.int32),
        ],
        compiler_params=params(),
    )(covers, parts)
    sums = lax.all_to_all(sums, "col", 0, 0, tiled=True)

    half = 2 * LANES
    blocks = col_count * MOST * SEGS
    flops = 4 * tile_rows * half * blocks * LANES
    edge = jax.ShapeDtypeStruct((2 * SWEEPS, tile_rows), F32)
    outer, left, right, stack, mean = pl.pallas_call(
        functools.partial(outer_kernel, first_slot),
        out_shape=(
            jax.ShapeDtypeStruct((tile_rows, half), F32),
            edge,
            edge,
            jax.ShapeDtypeStruct((blocks, 2 * tile_rows, LANES), BF16),
            jax.ShapeDtypeStruct((8, LANES), F32),
        ),
        in_specs=[vmem()] * 3,
        out_specs=(vmem(),) * 5,
        scratch_shapes=[pltpu.VMEM((half, 2 * tile_rows), F32)],
        compiler_params=params(),
        cost_estimate=pl.CostEstimate(flops=flops, transcendentals=0, bytes_accessed=1 << 20),
    )(parts, sums, ground_level_map)
    from_left = shift(right, "col", 1)
    from_right = shift(left, "col", -1)
    inside = tile_columns - half
    inner = pl.pallas_call(
        functools.partial(inner_kernel, first_slot),
        out_shape=jax.ShapeDtypeStruct((tile_rows, inside), F32),
        in_specs=[vmem()] * 4,
        out_specs=vmem(),
        scratch_shapes=[pltpu.VMEM((inside, 2 * tile_rows), F32)],
        compiler_params=params(),
        cost_estimate=pl.CostEstimate(flops=flops, transcendentals=0, bytes_accessed=1 << 20),
    )(parts, stack, mean, ground_level_map)

    strips = pl.pallas_call(
        strip_kernel,
        out_shape=jax.ShapeDtypeStruct((4 * SWEEPS, tile_columns + LANES), F32),
        in_specs=[vmem()] * 5,
        out_specs=vmem(),
        compiler_params=params(),
    )(outer, inner, ground_level_map, from_left, from_right)
    strips = lax.all_gather(strips, "row", axis=0, tiled=True)

    scratch = pltpu.VMEM((tile_rows + 16, tile_columns + 2 * LANES), F32)
    return pl.pallas_call(
        functools.partial(sweep_kernel, row_count, col_count),
        out_shape=jax.ShapeDtypeStruct((tile_rows, tile_columns), F32),
        in_specs=[vmem()] * 6,
        out_specs=vmem(),
        scratch_shapes=[scratch, scratch],
        compiler_params=params(),
    )(strips, from_left, from_right, outer, inner, ground_level_map)


def solution(mesh):
    in_specs = (
        P("row", "col"),
        P(("row", "col"), None),
        P(("row", "col")),
        P(("row", "col"), None, None),
        P(("row", "col"), None),
    )
    out_specs = P("row", "col")
    return jax.shard_map(body, mesh=mesh, in_specs=in_specs, out_specs=out_specs, check_vma=False)
```

```python
import functools

import jax
import jax.numpy as jnp
from jax import lax
from jax.experimental import pallas as pl
from jax.experimental.pallas import tpu as pltpu
from jax.sharding import PartitionSpec as P

SEGS = 4
SWEEPS = 4
MOST = 6
LANES = 128

spread = 4.0
tau_weight = 4.0
flow_gain = 8.0

F32 = jnp.float32
BF16 = jnp.bfloat16
VMEM_LIMIT = 24 * 1024 * 1024


def vmem():
    return pl.BlockSpec(memory_space=pltpu.VMEM)


def smem():
    return pl.BlockSpec(memory_space=pltpu.SMEM)


def params(limit=VMEM_LIMIT):
    return pltpu.CompilerParams(vmem_limit_bytes=limit)


def one_hot(cond):
    return jnp.where(cond, 1.0, 0.0).astype(BF16)


def pack_kernel(
    cover_hbm,
    ids_hbm,
    entry_hbm,
    place_hbm,
    ground_hbm,
    out_ref,
    ground_ref,
    cover_copy_ref,
    cover_ref,
    ids_ref,
    entry_ref,
    place_ref,
    used_ref,
    sems,
):
    owners, _, _ = out_ref.shape
    covers, bodies = cover_ref.shape
    copies = [
        pltpu.make_async_copy(source, target, sems.at[k])
        for k, (source, target) in enumerate(
            (
                (ids_hbm, ids_ref),
                (entry_hbm, entry_ref),
                (place_hbm, place_ref),
                (cover_hbm, cover_ref),
                (cover_hbm, cover_copy_ref),
                (ground_hbm, ground_ref),
            )
        )
    ]
    for copy in copies:
        copy.start()
    chunks = ids_ref.shape[0]
    sum_rows, count_rows = bodies * SEGS, bodies // 2
    first_slot = sum_rows + count_rows
    out_ref[:, first_slot:, :] = jnp.zeros((owners, MOST * 8, LANES), F32)
    for copy in copies:
        copy.wait()
    seg_iota = lax.broadcasted_iota(jnp.int32, (owners * sum_rows, LANES), 0)
    pair_iota = lax.broadcasted_iota(jnp.int32, (owners * count_rows, LANES), 0)
    lane_group = lax.broadcasted_iota(jnp.int32, (LANES, LANES), 0) // 16
    ids = [ids_ref[k : k + 1, :] for k in range(chunks)]
    by_pair = jnp.concatenate([one_hot(pair_iota == v // 8) for v in ids], axis=1)
    by_lane = jnp.concatenate([one_hot(lane_group == v % 8) for v in ids], axis=1)
    counts = lax.dot_general(
        by_pair, by_lane, (((1,), (1,)), ((), ())), preferred_element_type=F32
    )
    by_segment = jnp.concatenate([one_hot(seg_iota == v) for v in ids], axis=1)
    entries = entry_ref[...]
    high = entries.astype(BF16)
    low = (entries - high.astype(F32)).astype(BF16)
    both = jnp.dot(
        by_segment, jnp.concatenate([high, low], axis=1), preferred_element_type=F32
    )
    sums = both[:, :LANES] + both[:, LANES:]
    for owner in range(owners):
        out_ref[owner, :sum_rows, :] = sums[owner * sum_rows : (owner + 1) * sum_rows]
        out_ref[owner, sum_rows:first_slot, :] = counts[
            owner * count_rows : (owner + 1) * count_rows
        ]
    for column in range(owners):
        used_ref[column] = 0
    for body_id in range(bodies):
        rows = place_ref[body_id]
        tile = jnp.concatenate(
            [
                rows[axis : axis + 1, s * LANES : (s + 1) * LANES]
                for axis in range(2)
                for s in range(SEGS)
            ],
            axis=0,
        )
        for k in range(covers):
            column = cover_ref[k, body_id]
            slot = used_ref[column]
            used_ref[column] = slot + 1
            out_ref[column, pl.ds(pl.multiple_of(first_slot + slot * 8, 8), 8), :] = tile


def owner_kernel(cover_ref, part_ref, out_ref, total_ref, used_ref):
    columns = out_ref.shape[0]
    covers, bodies = cover_ref.shape
    rows = total_ref.shape[0]
    total = part_ref[0, :rows, :]
    for source in range(1, part_ref.shape[0]):
        total = total + part_ref[source, :rows, :]
    total_ref[...] = total
    out_ref[...] = jnp.zeros_like(out_ref)
    for column in range(columns):
        used_ref[column] = 0
    for body_id in range(bodies):
        sums = total_ref[body_id * SEGS : (body_id + 1) * SEGS, :]
        row, lane = bodies * SEGS + body_id // 2, 64 * (body_id % 2)
        count = total_ref[row : row + 1, lane : lane + 64]
        for k in range(covers):
            column = cover_ref[k, body_id]
            slot = used_ref[column]
            used_ref[column] = slot + 1
            out_ref[column, pl.ds(slot * SEGS, SEGS), :] = sums
            out_ref[column, pl.ds(MOST * SEGS + slot, 1), :64] = count


def lorentz(base, step):
    distance = base + step
    return 1.0 / (1.0 + distance * distance)


def cell_base(origin, coord):
    index = lax.broadcasted_iota(jnp.int32, (16, LANES), 0).astype(F32) * (1.0 / spread)
    return index - (coord - origin) * (1.0 / spread)


def column_block(place_ref, owner, row, origin, starts):
    parts = []
    for s in range(SEGS):
        base = cell_base(origin, place_ref[owner, row + SEGS + s : row + SEGS + s + 1, :])
        parts.append(
            jnp.concatenate(
                [
                    lorentz(base, (start + j) / spread).astype(BF16)
                    for start in starts
                    for j in range(0, LANES, 16)
                ],
                axis=0,
            )
        )
    return jnp.concatenate(parts, axis=1)


def times_stack(columns, stack):
    return lax.dot_general(
        columns, stack, (((1,), (1,)), ((), ())), preferred_element_type=F32
    )


def surface(acc, mean, ground):
    tile_rows = ground.shape[0]
    num = jnp.transpose(acc[:, :tile_rows])
    den = jnp.transpose(acc[:, tile_rows:])
    depth = (num + (mean - ground) * den) / (den + tau_weight)
    return jnp.maximum(depth, 0.0)


def outer_kernel(
    first_slot, place_ref, sums_ref, ground_ref, depth_ref, left_ref, right_ref, stack_ref, mean_ref, acc_ref
):
    tile_rows, tile_columns = ground_ref.shape
    owners = sums_ref.shape[0]
    row_origin = (lax.axis_index("row") * tile_rows).astype(F32)
    col_origin = (lax.axis_index("col") * tile_columns).astype(F32)
    elev = jnp.sum(sums_ref[:, : MOST * SEGS, :], axis=0)
    count = jnp.sum(sums_ref[:, MOST * SEGS : MOST * SEGS + 8, :], axis=0)
    elev = jnp.sum(jnp.sum(elev, axis=0, keepdims=True), axis=1, keepdims=True)
    count = jnp.sum(jnp.sum(count, axis=0, keepdims=True), axis=1, keepdims=True)
    mean = elev / jnp.maximum(count * (LANES / 16), 1.0)
    mean_ref[...] = jnp.broadcast_to(mean, mean_ref.shape)
    acc_ref[...] = jnp.zeros_like(acc_ref)
    starts = (0, tile_columns - LANES)

    @pl.loop(0, owners)
    def _(owner):
        for slot in range(MOST):
            row = first_slot + slot * 8
            blocks = []
            for s in range(SEGS):
                here = sums_ref[owner, MOST * SEGS + slot : MOST * SEGS + slot + 1, s * 16 : s * 16 + 1]
                part = sums_ref[owner, slot * SEGS + s : slot * SEGS + s + 1, :] - mean * here
                weight = jnp.broadcast_to(here, (16, LANES))
                part = jnp.broadcast_to(part, (16, LANES))
                base = cell_base(row_origin, place_ref[owner, row + s : row + s + 1, :])
                values = [lorentz(base, i / spread) for i in range(0, tile_rows, 16)]
                block = jnp.concatenate(
                    [(v * part).astype(BF16) for v in values]
                    + [(v * weight).astype(BF16) for v in values],
                    axis=0,
                )
                stack_ref[owner * (MOST * SEGS) + slot * SEGS + s] = block
                blocks.append(block)
            columns = column_block(place_ref, owner, row, col_origin, starts)
            acc_ref[...] += times_stack(columns, jnp.concatenate(blocks, axis=1))

    ground = jnp.concatenate(
        [ground_ref[:, start : start + LANES] for start in starts], axis=1
    )
    depth = surface(acc_ref[...], mean, ground)
    depth_ref[...] = depth
    for out_ref, start, pick in ((left_ref, 0, 0), (right_ref, LANES, LANES - SWEEPS)):
        for k, values in enumerate((depth, ground)):
            out_ref[k * SWEEPS : (k + 1) * SWEEPS, :] = jnp.transpose(
                values[:, start : start + LANES]
            )[pick : pick + SWEEPS]


def inner_kernel(first_slot, place_ref, stack_ref, mean_ref, ground_ref, depth_ref, acc_ref):
    tile_columns = ground_ref.shape[1]
    owners = place_ref.shape[0]
    col_origin = (lax.axis_index("col") * tile_columns).astype(F32)
    acc_ref[...] = jnp.zeros_like(acc_ref)
    starts = tuple(range(LANES, tile_columns - LANES, LANES))

    @pl.loop(0, owners)
    def _(owner):
        for slot in range(MOST):
            columns = column_block(place_ref, owner, first_slot + slot * 8, col_origin, starts)
            stack = jnp.concatenate(
                [stack_ref[owner * (MOST * SEGS) + slot * SEGS + s] for s in range(SEGS)], axis=1
            )
            acc_ref[...] += times_stack(columns, stack)

    ground = ground_ref[:, LANES : tile_columns - LANES]
    depth_ref[...] = surface(acc_ref[...], mean_ref[0:1, 0:1], ground)


def paste(outer, inner):
    return jnp.concatenate([outer[:, :LANES], inner, outer[:, LANES:]], axis=1)


def strip_kernel(outer_ref, inner_ref, ground_ref, left_ref, right_ref, strip_ref):
    tile_rows, tile_columns = ground_ref.shape
    sides = jnp.concatenate(
        [left_ref[:SWEEPS], right_ref[:SWEEPS], left_ref[SWEEPS:], right_ref[SWEEPS:]], axis=0
    )
    sides = jnp.transpose(sides)
    row = 0
    for k in range(2):
        for first in (0, tile_rows - SWEEPS):
            rows = slice(first, first + SWEEPS)
            if k == 0:
                main = paste(outer_ref[rows, :], inner_ref[rows, :])
            else:
                main = ground_ref[rows, :]
            strip_ref[row : row + SWEEPS, :tile_columns] = main
            strip_ref[row : row + SWEEPS, tile_columns:] = jnp.concatenate(
                [
                    sides[rows, 2 * SWEEPS * k : 2 * SWEEPS * (k + 1)],
                    jnp.zeros((SWEEPS, LANES - 2 * SWEEPS), F32),
                ],
                axis=1,
            )
            row += SWEEPS


def neighbour_rows(strip_ref, row_count):
    me = lax.axis_index("row")
    block = 4 * SWEEPS
    above = pl.multiple_of(jnp.maximum(me - 1, 0) * block, block)
    below = pl.multiple_of(jnp.minimum(me + 1, row_count - 1) * block, block)
    above = strip_ref[pl.ds(above, block), :]
    below = strip_ref[pl.ds(below, block), :]
    return (
        above[SWEEPS : 2 * SWEEPS],
        below[:SWEEPS],
        above[3 * SWEEPS :],
        below[2 * SWEEPS : 3 * SWEEPS],
    )


def sweep_kernel(
    row_count,
    col_count,
    strip_ref,
    left_ref,
    right_ref,
    outer_ref,
    inner_ref,
    ground_ref,
    out_ref,
    height_ref,
    land_ref,
):
    tile_rows, tile_columns = ground_ref.shape
    rows, cols = height_ref.shape
    depth_up, depth_down, ground_up, ground_down = neighbour_rows(strip_ref, row_count)
    sides = jnp.transpose(jnp.concatenate([left_ref[...], right_ref[...]], axis=0))
    blank = cols - tile_columns - 2 * SWEEPS

    def spare(left, right):
        return jnp.concatenate([right, jnp.zeros((right.shape[0], blank), F32), left], axis=1)

    for ref, up, down, k in (
        (height_ref, depth_up, depth_down, 0),
        (land_ref, ground_up, ground_down, SWEEPS),
    ):
        if k == 0:
            ref[:tile_rows, :LANES] = outer_ref[:, :LANES]
            ref[:tile_rows, LANES : tile_columns - LANES] = inner_ref[...]
            ref[:tile_rows, tile_columns - LANES : tile_columns] = outer_ref[:, LANES:]
        else:
            ref[:tile_rows, :tile_columns] = ground_ref[...]
        ref[tile_rows:, :tile_columns] = jnp.concatenate(
            [down[:, :tile_columns], up[:, :tile_columns]], axis=0
        )
        left = sides[:, k : k + SWEEPS]
        right = sides[:, 2 * SWEEPS + k : 3 * SWEEPS + k]
        ref[:tile_rows, tile_columns:] = spare(left, right)
        corner = jnp.concatenate([down[:, tile_columns:], up[:, tile_columns:]], axis=0)
        ref[tile_rows:, tile_columns:] = spare(
            corner[:, :SWEEPS], corner[:, SWEEPS : 2 * SWEEPS]
        )

    row_id = lax.broadcasted_iota(jnp.int32, (rows, 1), 0)
    row_id = jnp.where(row_id < tile_rows + SWEEPS, row_id, row_id - rows)
    row_id = row_id + lax.axis_index("row") * tile_rows
    col_id = lax.broadcasted_iota(jnp.int32, (1, cols), 1)
    col_id = jnp.where(col_id < tile_columns + LANES // 2, col_id, col_id - cols)
    col_id = col_id + lax.axis_index("col") * tile_columns
    grid_rows, grid_cols = tile_rows * row_count, tile_columns * col_count
    land = land_ref[...]
    gain_down = jnp.where((row_id >= 0) & (row_id < grid_rows - 1), flow_gain, 0.0)
    gain_right = jnp.where((col_id >= 0) & (col_id < grid_cols - 1), flow_gain, 0.0)
    down = gain_down / (1.0 + jnp.abs(land - pltpu.roll(land, rows - 1, 0)))
    right = gain_right / (1.0 + jnp.abs(land - pltpu.roll(land, cols - 1, 1)))
    up = pltpu.roll(down, 1, 0)
    left = pltpu.roll(right, 1, 1)
    scale = 1.0 / (1.0 + up + down + left + right)
    up, down, left, right = up * scale, down * scale, left * scale, right * scale
    height = height_ref[...]
    for _ in range(SWEEPS):
        height = (
            height * scale
            + up * pltpu.roll(height, 1, 0)
            + down * pltpu.roll(height, rows - 1, 0)
            + left * pltpu.roll(height, 1, 1)
            + right * pltpu.roll(height, cols - 1, 1)
        )
    out_ref[...] = height[:tile_rows, :tile_columns]


def shift(values, axis, step):
    count = lax.axis_size(axis)
    return lax.ppermute(values, axis, [(i, (i + step) % count) for i in range(count)])


def body(
    ground_level_map,
    shoreline_altitude_entries,
    shoreline_piece_position,
    lake_panel_locations,
    spanned_patch_verticals,
):
    tile_rows, tile_columns = ground_level_map.shape
    col_count = lax.axis_size("col")
    row_count = lax.axis_size("row")
    records, _ = shoreline_altitude_entries.shape
    bodies, _ = spanned_patch_verticals.shape
    covers = spanned_patch_verticals.T
    first_slot = bodies * SEGS + bodies // 2
    hbm = pl.BlockSpec(memory_space=pltpu.HBM)

    parts, ground_level_map, covers = pl.pallas_call(
        pack_kernel,
        out_shape=(
            jax.ShapeDtypeStruct((col_count, first_slot + MOST * 8, LANES), F32),
            jax.ShapeDtypeStruct(ground_level_map.shape, F32),
            jax.ShapeDtypeStruct(covers.shape, jnp.int32),
        ),
        in_specs=[hbm] * 5,
        out_specs=(vmem(),) * 3,
        scratch_shapes=[
            pltpu.SMEM(covers.shape, jnp.int32),
            pltpu.VMEM((records // LANES, LANES), jnp.int32),
            pltpu.VMEM((records, LANES), F32),
            pltpu.VMEM(lake_panel_locations.shape, F32),
            pltpu.SMEM((col_count,), jnp.int32),
            pltpu.SemaphoreType.DMA((6,)),
        ],
        compiler_params=params(),
    )(
        *(
            pltpu.with_memory_space_constraint(value, pltpu.HBM)
            for value in (
                covers,
                shoreline_piece_position.reshape(records // LANES, LANES),
                shoreline_altitude_entries,
                lake_panel_locations,
                ground_level_map,
            )
        )
    )
    parts = lax.all_to_all(parts, "col", 0, 0, tiled=True)

    slot_rows = MOST * SEGS + 8
    sums = pl.pallas_call(
        owner_kernel,
        out_shape=jax.ShapeDtypeStruct((col_count, slot_rows, LANES), F32),
        in_specs=[smem(), vmem()],
        out_specs=vmem(),
        scratch_shapes=[
            pltpu.VMEM((first_slot, LANES), F32),
            pltpu.SMEM((col_count,), jnp.int32),
        ],
        compiler_params=params(),
    )(covers, parts)
    sums = lax.all_to_all(sums, "col", 0, 0, tiled=True)

    half = 2 * LANES
    blocks = col_count * MOST * SEGS
    flops = 4 * tile_rows * half * blocks * LANES
    edge = jax.ShapeDtypeStruct((2 * SWEEPS, tile_rows), F32)
    outer, left, right, stack, mean = pl.pallas_call(
        functools.partial(outer_kernel, first_slot),
        out_shape=(
            jax.ShapeDtypeStruct((tile_rows, half), F32),
            edge,
            edge,
            jax.ShapeDtypeStruct((blocks, 2 * tile_rows, LANES), BF16),
            jax.ShapeDtypeStruct((8, LANES), F32),
        ),
        in_specs=[vmem()] * 3,
        out_specs=(vmem(),) * 5,
        scratch_shapes=[pltpu.VMEM((half, 2 * tile_rows), F32)],
        compiler_params=params(),
        cost_estimate=pl.CostEstimate(flops=flops, transcendentals=0, bytes_accessed=1 << 20),
    )(parts, sums, ground_level_map)
    from_left = shift(right, "col", 1)
    from_right = shift(left, "col", -1)
    inside = tile_columns - half
    inner = pl.pallas_call(
        functools.partial(inner_kernel, first_slot),
        out_shape=jax.ShapeDtypeStruct((tile_rows, inside), F32),
        in_specs=[vmem()] * 4,
        out_specs=vmem(),
        scratch_shapes=[pltpu.VMEM((inside, 2 * tile_rows), F32)],
        compiler_params=params(),
        cost_estimate=pl.CostEstimate(flops=flops, transcendentals=0, bytes_accessed=1 << 20),
    )(parts, stack, mean, ground_level_map)

    strips = pl.pallas_call(
        strip_kernel,
        out_shape=jax.ShapeDtypeStruct((4 * SWEEPS, tile_columns + LANES), F32),
        in_specs=[vmem()] * 5,
        out_specs=vmem(),
        compiler_params=params(),
    )(outer, inner, ground_level_map, from_left, from_right)
    strips = lax.all_gather(strips, "row", axis=0, tiled=True)

    scratch = pltpu.VMEM((tile_rows + 2 * SWEEPS, tile_columns + LANES), F32)
    return pl.pallas_call(
        functools.partial(sweep_kernel, row_count, col_count),
        out_shape=jax.ShapeDtypeStruct((tile_rows, tile_columns), F32),
        in_specs=[vmem()] * 6,
        out_specs=vmem(),
        scratch_shapes=[scratch, scratch],
        compiler_params=params(),
    )(strips, from_left, from_right, outer, inner, ground_level_map)


def solution(mesh):
    in_specs = (
        P("row", "col"),
        P(("row", "col"), None),
        P(("row", "col")),
        P(("row", "col"), None, None),
        P(("row", "col"), None),
    )
    out_specs = P("row", "col")
    return jax.shard_map(body, mesh=mesh, in_specs=in_specs, out_specs=out_specs, check_vma=False)
```

```python
import functools

import jax
import jax.numpy as jnp
from jax import lax
from jax.experimental import pallas as pl
from jax.experimental.pallas import tpu as pltpu
from jax.sharding import PartitionSpec as P

SEGS = 4
SWEEPS = 4
MOST = 6
LANES = 128

spread = 4.0
tau_weight = 4.0
flow_gain = 8.0

F32 = jnp.float32
BF16 = jnp.bfloat16
VMEM_LIMIT = 24 * 1024 * 1024


def vmem():
    return pl.BlockSpec(memory_space=pltpu.VMEM)


def smem():
    return pl.BlockSpec(memory_space=pltpu.SMEM)


def params(limit=VMEM_LIMIT):
    return pltpu.CompilerParams(vmem_limit_bytes=limit)


def one_hot(cond):
    return jnp.where(cond, 1.0, 0.0).astype(BF16)


def pack_kernel(
    cover_hbm,
    ids_hbm,
    entry_hbm,
    place_hbm,
    ground_hbm,
    out_ref,
    ground_ref,
    cover_copy_ref,
    cover_ref,
    ids_ref,
    entry_ref,
    place_ref,
    used_ref,
    sems,
):
    owners, _, _ = out_ref.shape
    covers, bodies = cover_ref.shape
    copies = [
        pltpu.make_async_copy(source, target, sems.at[k])
        for k, (source, target) in enumerate(
            (
                (ids_hbm, ids_ref),
                (entry_hbm, entry_ref),
                (place_hbm, place_ref),
                (cover_hbm, cover_ref),
                (cover_hbm, cover_copy_ref),
                (ground_hbm, ground_ref),
            )
        )
    ]
    for copy in copies:
        copy.start()
    chunks = ids_ref.shape[0]
    sum_rows, count_rows = bodies * SEGS, bodies // 2
    first_slot = sum_rows + count_rows
    out_ref[:, first_slot:, :] = jnp.zeros((owners, MOST * 8, LANES), F32)
    for copy in copies:
        copy.wait()
    seg_iota = lax.broadcasted_iota(jnp.int32, (owners * sum_rows, LANES), 0)
    pair_iota = lax.broadcasted_iota(jnp.int32, (owners * count_rows, LANES), 0)
    lane_group = lax.broadcasted_iota(jnp.int32, (LANES, LANES), 0) // 16
    ids = [ids_ref[k : k + 1, :] for k in range(chunks)]
    by_pair = jnp.concatenate([one_hot(pair_iota == v // 8) for v in ids], axis=1)
    by_lane = jnp.concatenate([one_hot(lane_group == v % 8) for v in ids], axis=1)
    counts = lax.dot_general(
        by_pair, by_lane, (((1,), (1,)), ((), ())), preferred_element_type=F32
    )
    by_segment = jnp.concatenate([one_hot(seg_iota == v) for v in ids], axis=1)
    entries = entry_ref[...]
    high = entries.astype(BF16)
    low = (entries - high.astype(F32)).astype(BF16)
    both = jnp.dot(
        by_segment, jnp.concatenate([high, low], axis=1), preferred_element_type=F32
    )
    sums = both[:, :LANES] + both[:, LANES:]
    for owner in range(owners):
        out_ref[owner, :sum_rows, :] = sums[owner * sum_rows : (owner + 1) * sum_rows]
        out_ref[owner, sum_rows:first_slot, :] = counts[
            owner * count_rows : (owner + 1) * count_rows
        ]
    for column in range(owners):
        used_ref[column] = 0
    for body_id in range(bodies):
        rows = place_ref[body_id]
        tile = jnp.concatenate(
            [
                rows[axis : axis + 1, s * LANES : (s + 1) * LANES]
                for axis in range(2)
                for s in range(SEGS)
            ],
            axis=0,
        )
        for k in range(covers):
            column = cover_ref[k, body_id]
            slot = used_ref[column]
            used_ref[column] = slot + 1
            out_ref[column, pl.ds(pl.multiple_of(first_slot + slot * 8, 8), 8), :] = tile


def owner_kernel(cover_ref, part_ref, out_ref, total_ref, used_ref):
    columns = out_ref.shape[0]
    covers, bodies = cover_ref.shape
    rows = total_ref.shape[0]
    total = part_ref[0, :rows, :]
    for source in range(1, part_ref.shape[0]):
        total = total + part_ref[source, :rows, :]
    total_ref[...] = total
    out_ref[...] = jnp.zeros_like(out_ref)
    for column in range(columns):
        used_ref[column] = 0
    for body_id in range(bodies):
        sums = total_ref[body_id * SEGS : (body_id + 1) * SEGS, :]
        row, lane = bodies * SEGS + body_id // 2, 64 * (body_id % 2)
        count = total_ref[row : row + 1, lane : lane + 64]
        for k in range(covers):
            column = cover_ref[k, body_id]
            slot = used_ref[column]
            used_ref[column] = slot + 1
            out_ref[column, pl.ds(slot * SEGS, SEGS), :] = sums
            out_ref[column, pl.ds(MOST * SEGS + slot, 1), :64] = count
    for column in range(columns):
        out_ref[column, MOST * SEGS + MOST : MOST * SEGS + MOST + 1, :] = jnp.full(
            (1, LANES), used_ref[column].astype(F32), F32
        )


def lorentz(base, step):
    distance = base + step
    return 1.0 / (1.0 + distance * distance)


def cell_base(origin, coord):
    index = lax.broadcasted_iota(jnp.int32, (16, LANES), 0).astype(F32) * (1.0 / spread)
    return index - (coord - origin) * (1.0 / spread)


def column_block(place_ref, owner, row, origin, starts):
    parts = []
    for s in range(SEGS):
        base = cell_base(origin, place_ref[owner, row + SEGS + s : row + SEGS + s + 1, :])
        parts.append(
            jnp.concatenate(
                [
                    lorentz(base, (start + j) / spread).astype(BF16)
                    for start in starts
                    for j in range(0, LANES, 16)
                ],
                axis=0,
            )
        )
    return jnp.concatenate(parts, axis=1)


def times_stack(columns, stack):
    return lax.dot_general(
        columns, stack, (((1,), (1,)), ((), ())), preferred_element_type=F32
    )


def surface(acc, mean, ground):
    tile_rows = ground.shape[0]
    num = jnp.transpose(acc[:, :tile_rows])
    den = jnp.transpose(acc[:, tile_rows:])
    depth = (num + (mean - ground) * den) / (den + tau_weight)
    return jnp.maximum(depth, 0.0)


def for_used_slots(owners, codes, run):
    for group, code in enumerate(codes):

        @pl.loop(0, min(8, owners - 8 * group))
        def _(k):
            used = lax.shift_right_logical(code, 3 * k) & 7
            for slots in range(2, MOST + 1, 2):

                @pl.when((used <= slots) & (used > slots - 2))
                def _():
                    run(8 * group + k, slots)


def outer_kernel(
    first_slot, place_ref, sums_ref, ground_ref, depth_ref, left_ref, right_ref, stack_ref, mean_ref, acc_ref
):
    tile_rows, tile_columns = ground_ref.shape
    owners = sums_ref.shape[0]
    row_origin = (lax.axis_index("row") * tile_rows).astype(F32)
    col_origin = (lax.axis_index("col") * tile_columns).astype(F32)
    elev = jnp.sum(sums_ref[:, : MOST * SEGS, :], axis=0)
    count = jnp.sum(sums_ref[:, MOST * SEGS : MOST * SEGS + MOST, :], axis=0)
    elev = jnp.sum(jnp.sum(elev, axis=0, keepdims=True), axis=1, keepdims=True)
    count = jnp.sum(jnp.sum(count, axis=0, keepdims=True), axis=1, keepdims=True)
    mean = elev / jnp.maximum(count * (LANES / 16), 1.0)
    mean_ref[...] = jnp.broadcast_to(mean, mean_ref.shape)
    codes = []
    for group in range((owners + 7) // 8):
        code = jnp.zeros((1, 1), F32)
        for owner in range(8 * group, min(8 * group + 8, owners)):
            used = sums_ref[owner, MOST * SEGS + MOST : MOST * SEGS + MOST + 1, 0:1]
            code = code + used * (8.0 ** (owner % 8))
        mean_ref[group + 1 : group + 2, :] = jnp.broadcast_to(code, (1, LANES))
        codes.append(jnp.max(code).astype(jnp.int32))
    acc_ref[...] = jnp.zeros_like(acc_ref)
    starts = (0, tile_columns - LANES)

    def run(owner, slots):
        for slot in range(slots):
            row = first_slot + slot * 8
            blocks = []
            for s in range(SEGS):
                here = sums_ref[owner, MOST * SEGS + slot : MOST * SEGS + slot + 1, s * 16 : s * 16 + 1]
                part = sums_ref[owner, slot * SEGS + s : slot * SEGS + s + 1, :] - mean * here
                weight = jnp.broadcast_to(here, (16, LANES))
                part = jnp.broadcast_to(part, (16, LANES))
                base = cell_base(row_origin, place_ref[owner, row + s : row + s + 1, :])
                values = [lorentz(base, i / spread) for i in range(0, tile_rows, 16)]
                block = jnp.concatenate(
                    [(v * part).astype(BF16) for v in values]
                    + [(v * weight).astype(BF16) for v in values],
                    axis=0,
                )
                stack_ref[owner * (MOST * SEGS) + slot * SEGS + s] = block
                blocks.append(block)
            columns = column_block(place_ref, owner, row, col_origin, starts)
            acc_ref[...] += times_stack(columns, jnp.concatenate(blocks, axis=1))

    for_used_slots(owners, codes, run)
    ground = jnp.concatenate(
        [ground_ref[:, start : start + LANES] for start in starts], axis=1
    )
    depth = surface(acc_ref[...], mean, ground)
    depth_ref[...] = depth
    for out_ref, start, pick in ((left_ref, 0, 0), (right_ref, LANES, LANES - SWEEPS)):
        for k, values in enumerate((depth, ground)):
            out_ref[k * SWEEPS : (k + 1) * SWEEPS, :] = jnp.transpose(
                values[:, start : start + LANES]
            )[pick : pick + SWEEPS]


def inner_kernel(first_slot, place_ref, stack_ref, mean_ref, ground_ref, depth_ref, acc_ref):
    tile_columns = ground_ref.shape[1]
    owners = place_ref.shape[0]
    col_origin = (lax.axis_index("col") * tile_columns).astype(F32)
    acc_ref[...] = jnp.zeros_like(acc_ref)
    starts = tuple(range(LANES, tile_columns - LANES, LANES))
    codes = [
        jnp.max(mean_ref[group + 1 : group + 2, :]).astype(jnp.int32)
        for group in range((owners + 7) // 8)
    ]

    def run(owner, slots):
        for slot in range(slots):
            columns = column_block(place_ref, owner, first_slot + slot * 8, col_origin, starts)
            stack = jnp.concatenate(
                [stack_ref[owner * (MOST * SEGS) + slot * SEGS + s] for s in range(SEGS)], axis=1
            )
            acc_ref[...] += times_stack(columns, stack)

    for_used_slots(owners, codes, run)
    ground = ground_ref[:, LANES : tile_columns - LANES]
    depth_ref[...] = surface(acc_ref[...], mean_ref[0:1, 0:1], ground)


def paste(outer, inner):
    return jnp.concatenate([outer[:, :LANES], inner, outer[:, LANES:]], axis=1)


def strip_kernel(outer_ref, inner_ref, ground_ref, left_ref, right_ref, strip_ref):
    tile_rows, tile_columns = ground_ref.shape
    sides = jnp.concatenate(
        [left_ref[:SWEEPS], right_ref[:SWEEPS], left_ref[SWEEPS:], right_ref[SWEEPS:]], axis=0
    )
    sides = jnp.transpose(sides)
    row = 0
    for k in range(2):
        for first in (0, tile_rows - SWEEPS):
            rows = slice(first, first + SWEEPS)
            if k == 0:
                main = paste(outer_ref[rows, :], inner_ref[rows, :])
            else:
                main = ground_ref[rows, :]
            strip_ref[row : row + SWEEPS, :tile_columns] = main
            strip_ref[row : row + SWEEPS, tile_columns:] = jnp.concatenate(
                [
                    sides[rows, 2 * SWEEPS * k : 2 * SWEEPS * (k + 1)],
                    jnp.zeros((SWEEPS, LANES - 2 * SWEEPS), F32),
                ],
                axis=1,
            )
            row += SWEEPS


def neighbour_rows(strip_ref, row_count):
    me = lax.axis_index("row")
    block = 4 * SWEEPS
    above = pl.multiple_of(jnp.maximum(me - 1, 0) * block, block)
    below = pl.multiple_of(jnp.minimum(me + 1, row_count - 1) * block, block)
    above = strip_ref[pl.ds(above, block), :]
    below = strip_ref[pl.ds(below, block), :]
    return (
        above[SWEEPS : 2 * SWEEPS],
        below[:SWEEPS],
        above[3 * SWEEPS :],
        below[2 * SWEEPS : 3 * SWEEPS],
    )


def sweep_kernel(
    row_count,
    col_count,
    strip_ref,
    left_ref,
    right_ref,
    outer_ref,
    inner_ref,
    ground_ref,
    out_ref,
    height_ref,
    land_ref,
):
    tile_rows, tile_columns = ground_ref.shape
    rows, cols = height_ref.shape
    depth_up, depth_down, ground_up, ground_down = neighbour_rows(strip_ref, row_count)
    sides = jnp.transpose(jnp.concatenate([left_ref[...], right_ref[...]], axis=0))
    blank = cols - tile_columns - 2 * SWEEPS

    def spare(left, right):
        return jnp.concatenate([right, jnp.zeros((right.shape[0], blank), F32), left], axis=1)

    for ref, up, down, k in (
        (height_ref, depth_up, depth_down, 0),
        (land_ref, ground_up, ground_down, SWEEPS),
    ):
        if k == 0:
            ref[:tile_rows, :LANES] = outer_ref[:, :LANES]
            ref[:tile_rows, LANES : tile_columns - LANES] = inner_ref[...]
            ref[:tile_rows, tile_columns - LANES : tile_columns] = outer_ref[:, LANES:]
        else:
            ref[:tile_rows, :tile_columns] = ground_ref[...]
        ref[tile_rows:, :tile_columns] = jnp.concatenate(
            [down[:, :tile_columns], up[:, :tile_columns]], axis=0
        )
        left = sides[:, k : k + SWEEPS]
        right = sides[:, 2 * SWEEPS + k : 3 * SWEEPS + k]
        ref[:tile_rows, tile_columns:] = spare(left, right)
        corner = jnp.concatenate([down[:, tile_columns:], up[:, tile_columns:]], axis=0)
        ref[tile_rows:, tile_columns:] = spare(
            corner[:, :SWEEPS], corner[:, SWEEPS : 2 * SWEEPS]
        )

    row_id = lax.broadcasted_iota(jnp.int32, (rows, 1), 0)
    row_id = jnp.where(row_id < tile_rows + SWEEPS, row_id, row_id - rows)
    row_id = row_id + lax.axis_index("row") * tile_rows
    col_id = lax.broadcasted_iota(jnp.int32, (1, cols), 1)
    col_id = jnp.where(col_id < tile_columns + LANES // 2, col_id, col_id - cols)
    col_id = col_id + lax.axis_index("col") * tile_columns
    grid_rows, grid_cols = tile_rows * row_count, tile_columns * col_count
    land = land_ref[...]
    gain_down = jnp.where((row_id >= 0) & (row_id < grid_rows - 1), flow_gain, 0.0)
    gain_right = jnp.where((col_id >= 0) & (col_id < grid_cols - 1), flow_gain, 0.0)
    down = gain_down / (1.0 + jnp.abs(land - pltpu.roll(land, rows - 1, 0)))
    right = gain_right / (1.0 + jnp.abs(land - pltpu.roll(land, cols - 1, 1)))
    up = pltpu.roll(down, 1, 0)
    left = pltpu.roll(right, 1, 1)
    scale = 1.0 / (1.0 + up + down + left + right)
    up, down, left, right = up * scale, down * scale, left * scale, right * scale
    height = height_ref[...]
    for _ in range(SWEEPS):
        height = (
            height * scale
            + up * pltpu.roll(height, 1, 0)
            + down * pltpu.roll(height, rows - 1, 0)
            + left * pltpu.roll(height, 1, 1)
            + right * pltpu.roll(height, cols - 1, 1)
        )
    out_ref[...] = height[:tile_rows, :tile_columns]


def shift(values, axis, step):
    count = lax.axis_size(axis)
    return lax.ppermute(values, axis, [(i, (i + step) % count) for i in range(count)])


def body(
    ground_level_map,
    shoreline_altitude_entries,
    shoreline_piece_position,
    lake_panel_locations,
    spanned_patch_verticals,
):
    tile_rows, tile_columns = ground_level_map.shape
    col_count = lax.axis_size("col")
    row_count = lax.axis_size("row")
    records, _ = shoreline_altitude_entries.shape
    bodies, _ = spanned_patch_verticals.shape
    covers = spanned_patch_verticals.T
    first_slot = bodies * SEGS + bodies // 2
    hbm = pl.BlockSpec(memory_space=pltpu.HBM)

    parts, ground_level_map, covers = pl.pallas_call(
        pack_kernel,
        out_shape=(
            jax.ShapeDtypeStruct((col_count, first_slot + MOST * 8, LANES), F32),
            jax.ShapeDtypeStruct(ground_level_map.shape, F32),
            jax.ShapeDtypeStruct(covers.shape, jnp.int32),
        ),
        in_specs=[hbm] * 5,
        out_specs=(vmem(),) * 3,
        scratch_shapes=[
            pltpu.SMEM(covers.shape, jnp.int32),
            pltpu.VMEM((records // LANES, LANES), jnp.int32),
            pltpu.VMEM((records, LANES), F32),
            pltpu.VMEM(lake_panel_locations.shape, F32),
            pltpu.SMEM((col_count,), jnp.int32),
            pltpu.SemaphoreType.DMA((6,)),
        ],
        compiler_params=params(),
    )(
        *(
            pltpu.with_memory_space_constraint(value, pltpu.HBM)
            for value in (
                covers,
                shoreline_piece_position.reshape(records // LANES, LANES),
                shoreline_altitude_entries,
                lake_panel_locations,
                ground_level_map,
            )
        )
    )
    parts = lax.all_to_all(parts, "col", 0, 0, tiled=True)

    slot_rows = MOST * SEGS + 8
    sums = pl.pallas_call(
        owner_kernel,
        out_shape=jax.ShapeDtypeStruct((col_count, slot_rows, LANES), F32),
        in_specs=[smem(), vmem()],
        out_specs=vmem(),
        scratch_shapes=[
            pltpu.VMEM((first_slot, LANES), F32),
            pltpu.SMEM((col_count,), jnp.int32),
        ],
        compiler_params=params(),
    )(covers, parts)
    sums = lax.all_to_all(sums, "col", 0, 0, tiled=True)

    half = 2 * LANES
    blocks = col_count * MOST * SEGS
    flops = 4 * tile_rows * half * blocks * LANES
    edge = jax.ShapeDtypeStruct((2 * SWEEPS, tile_rows), F32)
    outer, left, right, stack, mean = pl.pallas_call(
        functools.partial(outer_kernel, first_slot),
        out_shape=(
            jax.ShapeDtypeStruct((tile_rows, half), F32),
            edge,
            edge,
            jax.ShapeDtypeStruct((blocks, 2 * tile_rows, LANES), BF16),
            jax.ShapeDtypeStruct((8, LANES), F32),
        ),
        in_specs=[vmem()] * 3,
        out_specs=(vmem(),) * 5,
        scratch_shapes=[pltpu.VMEM((half, 2 * tile_rows), F32)],
        compiler_params=params(),
        cost_estimate=pl.CostEstimate(flops=flops, transcendentals=0, bytes_accessed=1 << 20),
    )(parts, sums, ground_level_map)
    from_left = shift(right, "col", 1)
    from_right = shift(left, "col", -1)
    inside = tile_columns - half
    inner = pl.pallas_call(
        functools.partial(inner_kernel, first_slot),
        out_shape=jax.ShapeDtypeStruct((tile_rows, inside), F32),
        in_specs=[vmem()] * 4,
        out_specs=vmem(),
        scratch_shapes=[pltpu.VMEM((inside, 2 * tile_rows), F32)],
        compiler_params=params(),
        cost_estimate=pl.CostEstimate(flops=flops, transcendentals=0, bytes_accessed=1 << 20),
    )(parts, stack, mean, ground_level_map)

    strips = pl.pallas_call(
        strip_kernel,
        out_shape=jax.ShapeDtypeStruct((4 * SWEEPS, tile_columns + LANES), F32),
        in_specs=[vmem()] * 5,
        out_specs=vmem(),
        compiler_params=params(),
    )(outer, inner, ground_level_map, from_left, from_right)
    strips = lax.all_gather(strips, "row", axis=0, tiled=True)

    scratch = pltpu.VMEM((tile_rows + 2 * SWEEPS, tile_columns + LANES), F32)
    return pl.pallas_call(
        functools.partial(sweep_kernel, row_count, col_count),
        out_shape=jax.ShapeDtypeStruct((tile_rows, tile_columns), F32),
        in_specs=[vmem()] * 6,
        out_specs=vmem(),
        scratch_shapes=[scratch, scratch],
        compiler_params=params(),
    )(strips, from_left, from_right, outer, inner, ground_level_map)


def solution(mesh):
    in_specs = (
        P("row", "col"),
        P(("row", "col"), None),
        P(("row", "col")),
        P(("row", "col"), None, None),
        P(("row", "col"), None),
    )
    out_specs = P("row", "col")
    return jax.shard_map(body, mesh=mesh, in_specs=in_specs, out_specs=out_specs, check_vma=False)
```

```python
import functools

import jax
import jax.numpy as jnp
from jax import lax
from jax.experimental import pallas as pl
from jax.experimental.pallas import tpu as pltpu
from jax.sharding import PartitionSpec as P

SEGS = 4
SWEEPS = 4
MOST = 6
LANES = 128

spread = 4.0
tau_weight = 4.0
flow_gain = 8.0

F32 = jnp.float32
BF16 = jnp.bfloat16
VMEM_LIMIT = 24 * 1024 * 1024


def vmem():
    return pl.BlockSpec(memory_space=pltpu.VMEM)


def smem():
    return pl.BlockSpec(memory_space=pltpu.SMEM)


def params(limit=VMEM_LIMIT):
    return pltpu.CompilerParams(vmem_limit_bytes=limit)


def one_hot(cond):
    return jnp.where(cond, 1.0, 0.0).astype(BF16)


def pack_kernel(
    cover_hbm,
    ids_hbm,
    entry_hbm,
    place_hbm,
    ground_hbm,
    out_ref,
    ground_ref,
    cover_copy_ref,
    cover_ref,
    ids_ref,
    entry_ref,
    place_ref,
    used_ref,
    sems,
):
    owners, _, _ = out_ref.shape
    covers, bodies = cover_ref.shape
    copies = [
        pltpu.make_async_copy(source, target, sems.at[k])
        for k, (source, target) in enumerate(
            (
                (ids_hbm, ids_ref),
                (entry_hbm, entry_ref),
                (place_hbm, place_ref),
                (cover_hbm, cover_ref),
                (cover_hbm, cover_copy_ref),
                (ground_hbm, ground_ref),
            )
        )
    ]
    for copy in copies:
        copy.start()
    chunks = ids_ref.shape[0]
    sum_rows, count_rows = bodies * SEGS, bodies // 2
    first_slot = sum_rows + count_rows
    out_ref[:, first_slot:, :] = jnp.zeros((owners, MOST * 8, LANES), F32)
    for copy in copies:
        copy.wait()
    seg_iota = lax.broadcasted_iota(jnp.int32, (owners * sum_rows, LANES), 0)
    pair_iota = lax.broadcasted_iota(jnp.int32, (owners * count_rows, LANES), 0)
    lane_group = lax.broadcasted_iota(jnp.int32, (LANES, LANES), 0) // 16
    ids = [ids_ref[k : k + 1, :] for k in range(chunks)]
    by_pair = jnp.concatenate([one_hot(pair_iota == v // 8) for v in ids], axis=1)
    by_lane = jnp.concatenate([one_hot(lane_group == v % 8) for v in ids], axis=1)
    counts = lax.dot_general(
        by_pair, by_lane, (((1,), (1,)), ((), ())), preferred_element_type=F32
    )
    by_segment = jnp.concatenate([one_hot(seg_iota == v) for v in ids], axis=1)
    entries = entry_ref[...]
    high = entries.astype(BF16)
    low = (entries - high.astype(F32)).astype(BF16)
    both = jnp.dot(
        by_segment, jnp.concatenate([high, low], axis=1), preferred_element_type=F32
    )
    sums = both[:, :LANES] + both[:, LANES:]
    for owner in range(owners):
        out_ref[owner, :sum_rows, :] = sums[owner * sum_rows : (owner + 1) * sum_rows]
        out_ref[owner, sum_rows:first_slot, :] = counts[
            owner * count_rows : (owner + 1) * count_rows
        ]
    for column in range(owners):
        used_ref[column] = 0
    for body_id in range(bodies):
        rows = place_ref[body_id]
        tile = jnp.concatenate(
            [
                rows[axis : axis + 1, s * LANES : (s + 1) * LANES]
                for axis in range(2)
                for s in range(SEGS)
            ],
            axis=0,
        )
        for k in range(covers):
            column = cover_ref[k, body_id]
            slot = used_ref[column]
            used_ref[column] = slot + 1
            out_ref[column, pl.ds(pl.multiple_of(first_slot + slot * 8, 8), 8), :] = tile


def owner_kernel(cover_ref, part_ref, out_ref, total_ref, used_ref):
    columns = out_ref.shape[0]
    covers, bodies = cover_ref.shape
    rows = total_ref.shape[0]
    total = part_ref[0, :rows, :]
    for source in range(1, part_ref.shape[0]):
        total = total + part_ref[source, :rows, :]
    total_ref[...] = total
    out_ref[...] = jnp.zeros_like(out_ref)
    for column in range(columns):
        used_ref[column] = 0
    for body_id in range(bodies):
        sums = total_ref[body_id * SEGS : (body_id + 1) * SEGS, :]
        row, lane = bodies * SEGS + body_id // 2, 64 * (body_id % 2)
        count = total_ref[row : row + 1, lane : lane + 64]
        for k in range(covers):
            column = cover_ref[k, body_id]
            slot = used_ref[column]
            used_ref[column] = slot + 1
            out_ref[column, pl.ds(slot * SEGS, SEGS), :] = sums
            out_ref[column, pl.ds(MOST * SEGS + slot, 1), :64] = count
    for column in range(columns):
        out_ref[column, MOST * SEGS + MOST : MOST * SEGS + MOST + 1, :] = jnp.full(
            (1, LANES), used_ref[column].astype(F32), F32
        )


def lorentz(base, step):
    distance = base + step
    return 1.0 / (1.0 + distance * distance)


def cell_base(origin, coord):
    index = lax.broadcasted_iota(jnp.int32, (16, LANES), 0).astype(F32) * (1.0 / spread)
    return index - (coord - origin) * (1.0 / spread)


def column_block(place_ref, owner, row, origin, starts):
    parts = []
    for s in range(SEGS):
        base = cell_base(origin, place_ref[owner, row + SEGS + s : row + SEGS + s + 1, :])
        parts.append(
            jnp.concatenate(
                [
                    lorentz(base, (start + j) / spread).astype(BF16)
                    for start in starts
                    for j in range(0, LANES, 16)
                ],
                axis=0,
            )
        )
    return jnp.concatenate(parts, axis=1)


def times_stack(columns, stack):
    return lax.dot_general(
        columns, stack, (((1,), (1,)), ((), ())), preferred_element_type=F32
    )


def surface(acc, mean, ground):
    tile_rows = ground.shape[0]
    num = jnp.transpose(acc[:, :tile_rows])
    den = jnp.transpose(acc[:, tile_rows:])
    depth = (num + (mean - ground) * den) / (den + tau_weight)
    return jnp.maximum(depth, 0.0)


def for_used_slots(owners, codes, run):
    for group, code in enumerate(codes):

        @pl.loop(0, min(8, owners - 8 * group))
        def _(k):
            used = lax.shift_right_logical(code, 3 * k) & 7
            for slots in range(2, MOST + 1, 2):

                @pl.when((used <= slots) & (used > slots - 2))
                def _():
                    run(8 * group + k, slots)


def outer_kernel(
    first_slot, place_ref, sums_ref, ground_ref, depth_ref, left_ref, right_ref, stack_ref, mean_ref, acc_ref
):
    tile_rows, tile_columns = ground_ref.shape
    owners = sums_ref.shape[0]
    row_origin = (lax.axis_index("row") * tile_rows).astype(F32)
    col_origin = (lax.axis_index("col") * tile_columns).astype(F32)
    elev = jnp.sum(sums_ref[:, : MOST * SEGS, :], axis=0)
    count = jnp.sum(sums_ref[:, MOST * SEGS : MOST * SEGS + MOST, :], axis=0)
    elev = jnp.sum(jnp.sum(elev, axis=0, keepdims=True), axis=1, keepdims=True)
    count = jnp.sum(jnp.sum(count, axis=0, keepdims=True), axis=1, keepdims=True)
    mean = elev / jnp.maximum(count * (LANES / 16), 1.0)
    mean_ref[...] = jnp.broadcast_to(mean, mean_ref.shape)
    codes = []
    for group in range((owners + 7) // 8):
        code = jnp.zeros((1, 1), F32)
        for owner in range(8 * group, min(8 * group + 8, owners)):
            used = sums_ref[owner, MOST * SEGS + MOST : MOST * SEGS + MOST + 1, 0:1]
            code = code + used * (8.0 ** (owner % 8))
        mean_ref[group + 1 : group + 2, :] = jnp.broadcast_to(code, (1, LANES))
        codes.append(jnp.max(code).astype(jnp.int32))
    acc_ref[...] = jnp.zeros_like(acc_ref)
    starts = (0, tile_columns - LANES)

    def run(owner, slots):
        for slot in range(slots):
            row = first_slot + slot * 8
            blocks = []
            for s in range(SEGS):
                here = sums_ref[owner, MOST * SEGS + slot : MOST * SEGS + slot + 1, s * 16 : s * 16 + 1]
                part = sums_ref[owner, slot * SEGS + s : slot * SEGS + s + 1, :] - mean * here
                weight = jnp.broadcast_to(here, (16, LANES))
                part = jnp.broadcast_to(part, (16, LANES))
                base = cell_base(row_origin, place_ref[owner, row + s : row + s + 1, :])
                values = [lorentz(base, i / spread) for i in range(0, tile_rows, 16)]
                block = jnp.concatenate(
                    [(v * part).astype(BF16) for v in values]
                    + [(v * weight).astype(BF16) for v in values],
                    axis=0,
                )
                stack_ref[owner * (MOST * SEGS) + slot * SEGS + s] = block
                blocks.append(block)
            columns = column_block(place_ref, owner, row, col_origin, starts)
            acc_ref[...] += times_stack(columns, jnp.concatenate(blocks, axis=1))

    for_used_slots(owners, codes, run)
    ground = jnp.concatenate(
        [ground_ref[:, start : start + LANES] for start in starts], axis=1
    )
    depth = surface(acc_ref[...], mean, ground)
    depth_ref[...] = depth
    for out_ref, start, pick in ((left_ref, 0, 0), (right_ref, LANES, LANES - SWEEPS)):
        for k, values in enumerate((depth, ground)):
            out_ref[k * SWEEPS : (k + 1) * SWEEPS, :] = jnp.transpose(
                values[:, start : start + LANES]
            )[pick : pick + SWEEPS]


def inner_kernel(first_slot, place_ref, stack_ref, mean_ref, ground_ref, depth_ref, acc_ref):
    tile_columns = ground_ref.shape[1]
    owners = place_ref.shape[0]
    col_origin = (lax.axis_index("col") * tile_columns).astype(F32)
    acc_ref[...] = jnp.zeros_like(acc_ref)
    starts = tuple(range(LANES, tile_columns - LANES, LANES))
    codes = [
        jnp.max(mean_ref[group + 1 : group + 2, :]).astype(jnp.int32)
        for group in range((owners + 7) // 8)
    ]

    def run(owner, slots):
        for slot in range(slots):
            columns = column_block(place_ref, owner, first_slot + slot * 8, col_origin, starts)
            stack = jnp.concatenate(
                [stack_ref[owner * (MOST * SEGS) + slot * SEGS + s] for s in range(SEGS)], axis=1
            )
            acc_ref[...] += times_stack(columns, stack)

    for_used_slots(owners, codes, run)
    ground = ground_ref[:, LANES : tile_columns - LANES]
    depth_ref[...] = surface(acc_ref[...], mean_ref[0:1, 0:1], ground)


def extend_kernel(
    outer_ref, inner_ref, ground_ref, left_ref, right_ref, height_ref, land_ref, top_ref, bottom_ref
):
    tile_rows, tile_columns = ground_ref.shape
    sides = jnp.transpose(jnp.concatenate([left_ref[...], right_ref[...]], axis=0))
    blank = jnp.zeros((tile_rows, LANES - 2 * SWEEPS), F32)
    height_ref[:, :LANES] = outer_ref[:, :LANES]
    height_ref[:, LANES : tile_columns - LANES] = inner_ref[...]
    height_ref[:, tile_columns - LANES : tile_columns] = outer_ref[:, LANES:]
    land_ref[:, :tile_columns] = ground_ref[...]
    for k, ref in enumerate((height_ref, land_ref)):
        left = sides[:, k * SWEEPS : (k + 1) * SWEEPS]
        right = sides[:, (2 + k) * SWEEPS : (3 + k) * SWEEPS]
        ref[:, tile_columns:] = jnp.concatenate([right, blank, left], axis=1)
        rows = slice(k * SWEEPS, (k + 1) * SWEEPS)
        top_ref[rows, :] = ref[:SWEEPS, :]
        bottom_ref[rows, :] = ref[tile_rows - SWEEPS :, :]


def relax(height, land, row_id, row_count, col_count, tile_rows, tile_columns):
    rows, cols = height.shape
    row_id = row_id + lax.axis_index("row") * tile_rows
    col_id = lax.broadcasted_iota(jnp.int32, (1, cols), 1)
    col_id = jnp.where(col_id < tile_columns + LANES // 2, col_id, col_id - cols)
    col_id = col_id + lax.axis_index("col") * tile_columns
    grid_rows, grid_cols = tile_rows * row_count, tile_columns * col_count
    gain_down = jnp.where((row_id >= 0) & (row_id < grid_rows - 1), flow_gain, 0.0)
    gain_right = jnp.where((col_id >= 0) & (col_id < grid_cols - 1), flow_gain, 0.0)
    down = gain_down / (1.0 + jnp.abs(land - pltpu.roll(land, rows - 1, 0)))
    right = gain_right / (1.0 + jnp.abs(land - pltpu.roll(land, cols - 1, 1)))
    up = pltpu.roll(down, 1, 0)
    left = pltpu.roll(right, 1, 1)
    scale = 1.0 / (1.0 + up + down + left + right)
    up, down, left, right = up * scale, down * scale, left * scale, right * scale
    for _ in range(SWEEPS):
        height = (
            height * scale
            + up * pltpu.roll(height, 1, 0)
            + down * pltpu.roll(height, rows - 1, 0)
            + left * pltpu.roll(height, 1, 1)
            + right * pltpu.roll(height, cols - 1, 1)
        )
    return height


def middle_kernel(row_count, col_count, height_ref, land_ref, out_ref):
    tile_rows, tile_columns = out_ref.shape
    row_id = lax.broadcasted_iota(jnp.int32, (tile_rows, 1), 0)
    height = relax(
        height_ref[...], land_ref[...], row_id, row_count, col_count, tile_rows, tile_columns
    )
    out_ref[...] = height[:, :tile_columns]


def band_kernel(row_count, col_count, height_ref, land_ref, above_ref, below_ref, _, out_hbm, rows_ref, sems):
    tile_rows, tile_columns = out_hbm.shape
    keep = 16 - SWEEPS

    def bands(ref, k):
        halo = slice(k * SWEEPS, (k + 1) * SWEEPS)
        return jnp.concatenate(
            [above_ref[halo, :], ref[:keep, :], ref[tile_rows - keep :, :], below_ref[halo, :]],
            axis=0,
        )

    row_id = lax.broadcasted_iota(jnp.int32, (32, 1), 0)
    row_id = jnp.where(row_id < 16, row_id - SWEEPS, row_id - 16 + tile_rows - keep)
    height = relax(
        bands(height_ref, 0), bands(land_ref, 1), row_id, row_count, col_count, tile_rows, tile_columns
    )
    rows_ref[0] = height[SWEEPS : SWEEPS + 8, :tile_columns]
    rows_ref[1] = height[16 + SWEEPS : 24 + SWEEPS, :tile_columns]
    copies = [
        pltpu.make_async_copy(rows_ref.at[k], out_hbm.at[pl.ds(first, 8), :], sems.at[k])
        for k, first in enumerate((0, tile_rows - 8))
    ]
    for copy in copies:
        copy.start()
    for copy in copies:
        copy.wait()


def shift(values, axis, step):
    count = lax.axis_size(axis)
    return lax.ppermute(values, axis, [(i, (i + step) % count) for i in range(count)])


def body(
    ground_level_map,
    shoreline_altitude_entries,
    shoreline_piece_position,
    lake_panel_locations,
    spanned_patch_verticals,
):
    tile_rows, tile_columns = ground_level_map.shape
    col_count = lax.axis_size("col")
    row_count = lax.axis_size("row")
    records, _ = shoreline_altitude_entries.shape
    bodies, _ = spanned_patch_verticals.shape
    covers = spanned_patch_verticals.T
    first_slot = bodies * SEGS + bodies // 2
    hbm = pl.BlockSpec(memory_space=pltpu.HBM)

    parts, ground_level_map, covers = pl.pallas_call(
        pack_kernel,
        out_shape=(
            jax.ShapeDtypeStruct((col_count, first_slot + MOST * 8, LANES), F32),
            jax.ShapeDtypeStruct(ground_level_map.shape, F32),
            jax.ShapeDtypeStruct(covers.shape, jnp.int32),
        ),
        in_specs=[hbm] * 5,
        out_specs=(vmem(),) * 3,
        scratch_shapes=[
            pltpu.SMEM(covers.shape, jnp.int32),
            pltpu.VMEM((records // LANES, LANES), jnp.int32),
            pltpu.VMEM((records, LANES), F32),
            pltpu.VMEM(lake_panel_locations.shape, F32),
            pltpu.SMEM((col_count,), jnp.int32),
            pltpu.SemaphoreType.DMA((6,)),
        ],
        compiler_params=params(),
    )(
        *(
            pltpu.with_memory_space_constraint(value, pltpu.HBM)
            for value in (
                covers,
                shoreline_piece_position.reshape(records // LANES, LANES),
                shoreline_altitude_entries,
                lake_panel_locations,
                ground_level_map,
            )
        )
    )
    parts = lax.all_to_all(parts, "col", 0, 0, tiled=True)

    slot_rows = MOST * SEGS + 8
    sums = pl.pallas_call(
        owner_kernel,
        out_shape=jax.ShapeDtypeStruct((col_count, slot_rows, LANES), F32),
        in_specs=[smem(), vmem()],
        out_specs=vmem(),
        scratch_shapes=[
            pltpu.VMEM((first_slot, LANES), F32),
            pltpu.SMEM((col_count,), jnp.int32),
        ],
        compiler_params=params(),
    )(covers, parts)
    sums = lax.all_to_all(sums, "col", 0, 0, tiled=True)

    half = 2 * LANES
    blocks = col_count * MOST * SEGS
    flops = 4 * tile_rows * half * blocks * LANES
    edge = jax.ShapeDtypeStruct((2 * SWEEPS, tile_rows), F32)
    outer, left, right, stack, mean = pl.pallas_call(
        functools.partial(outer_kernel, first_slot),
        out_shape=(
            jax.ShapeDtypeStruct((tile_rows, half), F32),
            edge,
            edge,
            jax.ShapeDtypeStruct((blocks, 2 * tile_rows, LANES), BF16),
            jax.ShapeDtypeStruct((8, LANES), F32),
        ),
        in_specs=[vmem()] * 3,
        out_specs=(vmem(),) * 5,
        scratch_shapes=[pltpu.VMEM((half, 2 * tile_rows), F32)],
        compiler_params=params(),
        cost_estimate=pl.CostEstimate(flops=flops, transcendentals=0, bytes_accessed=1 << 20),
    )(parts, sums, ground_level_map)
    from_left = shift(right, "col", 1)
    from_right = shift(left, "col", -1)
    inside = tile_columns - half
    inner = pl.pallas_call(
        functools.partial(inner_kernel, first_slot),
        out_shape=jax.ShapeDtypeStruct((tile_rows, inside), F32),
        in_specs=[vmem()] * 4,
        out_specs=vmem(),
        scratch_shapes=[pltpu.VMEM((inside, 2 * tile_rows), F32)],
        compiler_params=params(),
        cost_estimate=pl.CostEstimate(flops=flops, transcendentals=0, bytes_accessed=1 << 20),
    )(parts, stack, mean, ground_level_map)

    wide = jax.ShapeDtypeStruct((tile_rows, tile_columns + LANES), F32)
    edge = jax.ShapeDtypeStruct((2 * SWEEPS, tile_columns + LANES), F32)
    height, land, top, bottom = pl.pallas_call(
        extend_kernel,
        out_shape=(wide, wide, edge, edge),
        in_specs=[vmem()] * 5,
        out_specs=(vmem(),) * 4,
        compiler_params=params(),
    )(outer, inner, ground_level_map, from_left, from_right)
    from_above = shift(bottom, "row", 1)
    from_below = shift(top, "row", -1)
    tile = jax.ShapeDtypeStruct((tile_rows, tile_columns), F32)
    depth = pl.pallas_call(
        functools.partial(middle_kernel, row_count, col_count),
        out_shape=tile,
        in_specs=[vmem()] * 2,
        out_specs=vmem(),
        compiler_params=params(),
        cost_estimate=pl.CostEstimate(
            flops=100 * tile_rows * tile_columns, transcendentals=0, bytes_accessed=1 << 22
        ),
    )(height, land)
    return pl.pallas_call(
        functools.partial(band_kernel, row_count, col_count),
        out_shape=tile,
        in_specs=[vmem()] * 4 + [hbm],
        out_specs=hbm,
        input_output_aliases={4: 0},
        scratch_shapes=[pltpu.VMEM((2, 8, tile_columns), F32), pltpu.SemaphoreType.DMA((2,))],
        compiler_params=params(),
    )(height, land, from_above, from_below, depth)


def solution(mesh):
    in_specs = (
        P("row", "col"),
        P(("row", "col"), None),
        P(("row", "col")),
        P(("row", "col"), None, None),
        P(("row", "col"), None),
    )
    out_specs = P("row", "col")
    return jax.shard_map(body, mesh=mesh, in_specs=in_specs, out_specs=out_specs, check_vma=False)
```

```python
import functools

import jax
import jax.numpy as jnp
from jax import lax
from jax.experimental import pallas as pl
from jax.experimental.pallas import tpu as pltpu
from jax.sharding import PartitionSpec as P

SEGS = 4
SWEEPS = 4
MOST = 6
LANES = 128

spread = 4.0
tau_weight = 4.0
flow_gain = 8.0

F32 = jnp.float32
BF16 = jnp.bfloat16
VMEM_LIMIT = 24 * 1024 * 1024


def vmem():
    return pl.BlockSpec(memory_space=pltpu.VMEM)


def smem():
    return pl.BlockSpec(memory_space=pltpu.SMEM)


def params(limit=VMEM_LIMIT):
    return pltpu.CompilerParams(vmem_limit_bytes=limit)


def one_hot(cond):
    return jnp.where(cond, 1.0, 0.0).astype(BF16)


def pack_kernel(
    cover_hbm,
    ids_hbm,
    entry_hbm,
    place_hbm,
    ground_hbm,
    out_ref,
    ground_ref,
    cover_copy_ref,
    cover_ref,
    ids_ref,
    entry_ref,
    place_ref,
    used_ref,
    sems,
):
    owners, _, _ = out_ref.shape
    covers, bodies = cover_ref.shape
    copies = [
        pltpu.make_async_copy(source, target, sems.at[k])
        for k, (source, target) in enumerate(
            (
                (ids_hbm, ids_ref),
                (entry_hbm, entry_ref),
                (place_hbm, place_ref),
                (cover_hbm, cover_ref),
                (cover_hbm, cover_copy_ref),
                (ground_hbm, ground_ref),
            )
        )
    ]
    for copy in copies:
        copy.start()
    chunks = ids_ref.shape[0]
    sum_rows, count_rows = bodies * SEGS, bodies // 2
    first_slot = sum_rows + count_rows
    out_ref[:, first_slot:, :] = jnp.zeros((owners, MOST * 8, LANES), F32)
    for copy in copies:
        copy.wait()
    seg_iota = lax.broadcasted_iota(jnp.int32, (owners * sum_rows, LANES), 0)
    pair_iota = lax.broadcasted_iota(jnp.int32, (owners * count_rows, LANES), 0)
    lane_group = lax.broadcasted_iota(jnp.int32, (LANES, LANES), 0) // 16
    ids = [ids_ref[k : k + 1, :] for k in range(chunks)]
    by_pair = jnp.concatenate([one_hot(pair_iota == v // 8) for v in ids], axis=1)
    by_lane = jnp.concatenate([one_hot(lane_group == v % 8) for v in ids], axis=1)
    counts = lax.dot_general(
        by_pair, by_lane, (((1,), (1,)), ((), ())), preferred_element_type=F32
    )
    by_segment = jnp.concatenate([one_hot(seg_iota == v) for v in ids], axis=1)
    entries = entry_ref[...]
    high = entries.astype(BF16)
    low = (entries - high.astype(F32)).astype(BF16)
    both = jnp.dot(
        by_segment, jnp.concatenate([high, low], axis=1), preferred_element_type=F32
    )
    sums = both[:, :LANES] + both[:, LANES:]
    for owner in range(owners):
        out_ref[owner, :sum_rows, :] = sums[owner * sum_rows : (owner + 1) * sum_rows]
        out_ref[owner, sum_rows:first_slot, :] = counts[
            owner * count_rows : (owner + 1) * count_rows
        ]
    for column in range(owners):
        used_ref[column] = 0
    for body_id in range(bodies):
        rows = place_ref[body_id]
        tile = jnp.concatenate(
            [
                rows[axis : axis + 1, s * LANES : (s + 1) * LANES]
                for axis in range(2)
                for s in range(SEGS)
            ],
            axis=0,
        )
        for k in range(covers):
            column = cover_ref[k, body_id]
            slot = used_ref[column]
            used_ref[column] = slot + 1
            out_ref[column, pl.ds(pl.multiple_of(first_slot + slot * 8, 8), 8), :] = tile


def owner_kernel(cover_ref, part_ref, out_ref, total_ref, used_ref):
    columns = out_ref.shape[0]
    covers, bodies = cover_ref.shape
    rows = total_ref.shape[0]
    total = part_ref[0, :rows, :]
    for source in range(1, part_ref.shape[0]):
        total = total + part_ref[source, :rows, :]
    total_ref[...] = total
    out_ref[...] = jnp.zeros_like(out_ref)
    for column in range(columns):
        used_ref[column] = 0
    for body_id in range(bodies):
        sums = total_ref[body_id * SEGS : (body_id + 1) * SEGS, :]
        row, lane = bodies * SEGS + body_id // 2, 64 * (body_id % 2)
        count = total_ref[row : row + 1, lane : lane + 64]
        for k in range(covers):
            column = cover_ref[k, body_id]
            slot = used_ref[column]
            used_ref[column] = slot + 1
            out_ref[column, pl.ds(slot * SEGS, SEGS), :] = sums
            out_ref[column, pl.ds(MOST * SEGS + slot, 1), :64] = count
    for column in range(columns):
        out_ref[column, MOST * SEGS + MOST : MOST * SEGS + MOST + 1, :] = jnp.full(
            (1, LANES), used_ref[column].astype(F32), F32
        )


def lorentz(base, step):
    distance = base + step
    return 1.0 / (1.0 + distance * distance)


def cell_base(origin, coord):
    index = lax.broadcasted_iota(jnp.int32, (16, LANES), 0).astype(F32) * (1.0 / spread)
    return index - (coord - origin) * (1.0 / spread)


def column_block(place_ref, owner, row, origin, starts):
    parts = []
    for s in range(SEGS):
        base = cell_base(origin, place_ref[owner, row + SEGS + s : row + SEGS + s + 1, :])
        parts.append(
            jnp.concatenate(
                [
                    lorentz(base, (start + j) / spread).astype(BF16)
                    for start in starts
                    for j in range(0, LANES, 16)
                ],
                axis=0,
            )
        )
    return jnp.concatenate(parts, axis=1)


def times_stack(columns, stack):
    return lax.dot_general(
        columns, stack, (((1,), (1,)), ((), ())), preferred_element_type=F32
    )


def surface(acc, mean, ground):
    tile_rows = ground.shape[0]
    num = jnp.transpose(acc[:, :tile_rows])
    den = jnp.transpose(acc[:, tile_rows:])
    depth = (num + (mean - ground) * den) / (den + tau_weight)
    return jnp.maximum(depth, 0.0)


def for_used_slots(owners, codes, run):
    for group, code in enumerate(codes):

        @pl.loop(0, min(8, owners - 8 * group))
        def _(k):
            used = lax.shift_right_logical(code, 3 * k) & 7
            for slots in range(2, MOST + 1, 2):

                @pl.when((used <= slots) & (used > slots - 2))
                def _():
                    run(8 * group + k, slots)


def outer_kernel(
    first_slot, place_ref, sums_ref, ground_ref, depth_ref, left_ref, right_ref, stack_ref, mean_ref, acc_ref
):
    tile_rows, tile_columns = ground_ref.shape
    owners = sums_ref.shape[0]
    row_origin = (lax.axis_index("row") * tile_rows).astype(F32)
    col_origin = (lax.axis_index("col") * tile_columns).astype(F32)
    elev = jnp.sum(sums_ref[:, : MOST * SEGS, :], axis=0)
    count = jnp.sum(sums_ref[:, MOST * SEGS : MOST * SEGS + MOST, :], axis=0)
    elev = jnp.sum(jnp.sum(elev, axis=0, keepdims=True), axis=1, keepdims=True)
    count = jnp.sum(jnp.sum(count, axis=0, keepdims=True), axis=1, keepdims=True)
    mean = elev / jnp.maximum(count * (LANES / 16), 1.0)
    mean_ref[...] = jnp.broadcast_to(mean, mean_ref.shape)
    codes = []
    for group in range((owners + 7) // 8):
        code = jnp.zeros((1, 1), F32)
        for owner in range(8 * group, min(8 * group + 8, owners)):
            used = sums_ref[owner, MOST * SEGS + MOST : MOST * SEGS + MOST + 1, 0:1]
            code = code + used * (8.0 ** (owner % 8))
        mean_ref[group + 1 : group + 2, :] = jnp.broadcast_to(code, (1, LANES))
        codes.append(jnp.max(code).astype(jnp.int32))
    acc_ref[...] = jnp.zeros_like(acc_ref)
    starts = (0, tile_columns - LANES)

    def run(owner, slots):
        for slot in range(slots):
            row = first_slot + slot * 8
            blocks = []
            for s in range(SEGS):
                here = sums_ref[owner, MOST * SEGS + slot : MOST * SEGS + slot + 1, s * 16 : s * 16 + 1]
                part = sums_ref[owner, slot * SEGS + s : slot * SEGS + s + 1, :] - mean * here
                weight = jnp.broadcast_to(here, (16, LANES))
                part = jnp.broadcast_to(part, (16, LANES))
                base = cell_base(row_origin, place_ref[owner, row + s : row + s + 1, :])
                values = [lorentz(base, i / spread) for i in range(0, tile_rows, 16)]
                block = jnp.concatenate(
                    [(v * part).astype(BF16) for v in values]
                    + [(v * weight).astype(BF16) for v in values],
                    axis=0,
                )
                stack_ref[owner * (MOST * SEGS) + slot * SEGS + s] = block
                blocks.append(block)
            columns = column_block(place_ref, owner, row, col_origin, starts)
            acc_ref[...] += times_stack(columns, jnp.concatenate(blocks, axis=1))

    for_used_slots(owners, codes, run)
    ground = jnp.concatenate(
        [ground_ref[:, start : start + LANES] for start in starts], axis=1
    )
    depth = surface(acc_ref[...], mean, ground)
    depth_ref[...] = depth
    for out_ref, start, pick in ((left_ref, 0, 0), (right_ref, LANES, LANES - SWEEPS)):
        for k, values in enumerate((depth, ground)):
            out_ref[k * SWEEPS : (k + 1) * SWEEPS, :] = jnp.transpose(
                values[:, start : start + LANES]
            )[pick : pick + SWEEPS]


def inner_kernel(first_slot, place_ref, stack_ref, mean_ref, ground_ref, depth_ref, acc_ref):
    tile_columns = ground_ref.shape[1]
    owners = place_ref.shape[0]
    col_origin = (lax.axis_index("col") * tile_columns).astype(F32)
    acc_ref[...] = jnp.zeros_like(acc_ref)
    starts = tuple(range(LANES, tile_columns - LANES, LANES))
    codes = [
        jnp.max(mean_ref[group + 1 : group + 2, :]).astype(jnp.int32)
        for group in range((owners + 7) // 8)
    ]

    def run(owner, slots):
        for slot in range(slots):
            columns = column_block(place_ref, owner, first_slot + slot * 8, col_origin, starts)
            stack = jnp.concatenate(
                [stack_ref[owner * (MOST * SEGS) + slot * SEGS + s] for s in range(SEGS)], axis=1
            )
            acc_ref[...] += times_stack(columns, stack)

    for_used_slots(owners, codes, run)
    ground = ground_ref[:, LANES : tile_columns - LANES]
    depth_ref[...] = surface(acc_ref[...], mean_ref[0:1, 0:1], ground)


def extend_kernel(
    outer_ref, inner_ref, ground_ref, left_ref, right_ref, height_ref, land_ref, top_ref, bottom_ref
):
    tile_rows, tile_columns = ground_ref.shape
    sides = jnp.transpose(jnp.concatenate([left_ref[...], right_ref[...]], axis=0))
    blank = jnp.zeros((tile_rows, LANES - 2 * SWEEPS), F32)
    height_ref[:, :LANES] = outer_ref[:, :LANES]
    height_ref[:, LANES : tile_columns - LANES] = inner_ref[...]
    height_ref[:, tile_columns - LANES : tile_columns] = outer_ref[:, LANES:]
    land_ref[:, :tile_columns] = ground_ref[...]
    for k, ref in enumerate((height_ref, land_ref)):
        left = sides[:, k * SWEEPS : (k + 1) * SWEEPS]
        right = sides[:, (2 + k) * SWEEPS : (3 + k) * SWEEPS]
        ref[:, tile_columns:] = jnp.concatenate([right, blank, left], axis=1)
        rows = slice(k * SWEEPS, (k + 1) * SWEEPS)
        top_ref[rows, :] = ref[:SWEEPS, :]
        bottom_ref[rows, :] = ref[tile_rows - SWEEPS :, :]


def relax(height, land, row_id, row_count, col_count, tile_rows, tile_columns):
    rows, cols = height.shape
    row_id = row_id + lax.axis_index("row") * tile_rows
    col_id = lax.broadcasted_iota(jnp.int32, (1, cols), 1)
    col_id = jnp.where(col_id < tile_columns + LANES // 2, col_id, col_id - cols)
    col_id = col_id + lax.axis_index("col") * tile_columns
    grid_rows, grid_cols = tile_rows * row_count, tile_columns * col_count
    gain_down = jnp.where((row_id >= 0) & (row_id < grid_rows - 1), flow_gain, 0.0)
    gain_right = jnp.where((col_id >= 0) & (col_id < grid_cols - 1), flow_gain, 0.0)
    down = gain_down / (1.0 + jnp.abs(land - pltpu.roll(land, rows - 1, 0)))
    right = gain_right / (1.0 + jnp.abs(land - pltpu.roll(land, cols - 1, 1)))
    up = pltpu.roll(down, 1, 0)
    left = pltpu.roll(right, 1, 1)
    scale = 1.0 / (1.0 + up + down + left + right)
    up, down, left, right = up * scale, down * scale, left * scale, right * scale
    for _ in range(SWEEPS):
        height = (
            height * scale
            + up * pltpu.roll(height, 1, 0)
            + down * pltpu.roll(height, rows - 1, 0)
            + left * pltpu.roll(height, 1, 1)
            + right * pltpu.roll(height, cols - 1, 1)
        )
    return height


def middle_kernel(row_count, col_count, height_ref, land_ref, out_ref):
    tile_rows, tile_columns = out_ref.shape
    row_id = lax.broadcasted_iota(jnp.int32, (tile_rows, 1), 0)
    height = relax(
        height_ref[...], land_ref[...], row_id, row_count, col_count, tile_rows, tile_columns
    )
    out_ref[...] = height[:, :tile_columns]


def band_kernel(
    row_count, col_count, height_ref, land_ref, above_ref, below_ref, middle_ref, out_hbm, rows_ref, sems
):
    tile_rows, tile_columns = out_hbm.shape
    keep = 16 - SWEEPS
    middle = pl.ds(8, tile_rows - 16)
    middle_copy = pltpu.make_async_copy(middle_ref.at[middle, :], out_hbm.at[middle, :], sems.at[2])
    middle_copy.start()

    def bands(ref, k):
        halo = slice(k * SWEEPS, (k + 1) * SWEEPS)
        return jnp.concatenate(
            [above_ref[halo, :], ref[:keep, :], ref[tile_rows - keep :, :], below_ref[halo, :]],
            axis=0,
        )

    row_id = lax.broadcasted_iota(jnp.int32, (32, 1), 0)
    row_id = jnp.where(row_id < 16, row_id - SWEEPS, row_id - 16 + tile_rows - keep)
    height = relax(
        bands(height_ref, 0), bands(land_ref, 1), row_id, row_count, col_count, tile_rows, tile_columns
    )
    rows_ref[0] = height[SWEEPS : SWEEPS + 8, :tile_columns]
    rows_ref[1] = height[16 + SWEEPS : 24 + SWEEPS, :tile_columns]
    copies = [
        pltpu.make_async_copy(rows_ref.at[k], out_hbm.at[pl.ds(first, 8), :], sems.at[k])
        for k, first in enumerate((0, tile_rows - 8))
    ]
    for copy in copies:
        copy.start()
    for copy in copies:
        copy.wait()
    middle_copy.wait()


def shift(values, axis, step):
    count = lax.axis_size(axis)
    return lax.ppermute(values, axis, [(i, (i + step) % count) for i in range(count)])


def body(
    ground_level_map,
    shoreline_altitude_entries,
    shoreline_piece_position,
    lake_panel_locations,
    spanned_patch_verticals,
):
    tile_rows, tile_columns = ground_level_map.shape
    col_count = lax.axis_size("col")
    row_count = lax.axis_size("row")
    records, _ = shoreline_altitude_entries.shape
    bodies, _ = spanned_patch_verticals.shape
    covers = spanned_patch_verticals.T
    first_slot = bodies * SEGS + bodies // 2
    hbm = pl.BlockSpec(memory_space=pltpu.HBM)

    parts, ground_level_map, covers = pl.pallas_call(
        pack_kernel,
        out_shape=(
            jax.ShapeDtypeStruct((col_count, first_slot + MOST * 8, LANES), F32),
            jax.ShapeDtypeStruct(ground_level_map.shape, F32),
            jax.ShapeDtypeStruct(covers.shape, jnp.int32),
        ),
        in_specs=[hbm] * 5,
        out_specs=(vmem(),) * 3,
        scratch_shapes=[
            pltpu.SMEM(covers.shape, jnp.int32),
            pltpu.VMEM((records // LANES, LANES), jnp.int32),
            pltpu.VMEM((records, LANES), F32),
            pltpu.VMEM(lake_panel_locations.shape, F32),
            pltpu.SMEM((col_count,), jnp.int32),
            pltpu.SemaphoreType.DMA((6,)),
        ],
        compiler_params=params(),
    )(
        *(
            pltpu.with_memory_space_constraint(value, pltpu.HBM)
            for value in (
                covers,
                shoreline_piece_position.reshape(records // LANES, LANES),
                shoreline_altitude_entries,
                lake_panel_locations,
                ground_level_map,
            )
        )
    )
    parts = lax.all_to_all(parts, "col", 0, 0, tiled=True)

    slot_rows = MOST * SEGS + 8
    sums = pl.pallas_call(
        owner_kernel,
        out_shape=jax.ShapeDtypeStruct((col_count, slot_rows, LANES), F32),
        in_specs=[smem(), vmem()],
        out_specs=vmem(),
        scratch_shapes=[
            pltpu.VMEM((first_slot, LANES), F32),
            pltpu.SMEM((col_count,), jnp.int32),
        ],
        compiler_params=params(),
    )(covers, parts)
    sums = lax.all_to_all(sums, "col", 0, 0, tiled=True)

    half = 2 * LANES
    blocks = col_count * MOST * SEGS
    flops = 4 * tile_rows * half * blocks * LANES
    edge = jax.ShapeDtypeStruct((2 * SWEEPS, tile_rows), F32)
    outer, left, right, stack, mean = pl.pallas_call(
        functools.partial(outer_kernel, first_slot),
        out_shape=(
            jax.ShapeDtypeStruct((tile_rows, half), F32),
            edge,
            edge,
            jax.ShapeDtypeStruct((blocks, 2 * tile_rows, LANES), BF16),
            jax.ShapeDtypeStruct((8, LANES), F32),
        ),
        in_specs=[vmem()] * 3,
        out_specs=(vmem(),) * 5,
        scratch_shapes=[pltpu.VMEM((half, 2 * tile_rows), F32)],
        compiler_params=params(),
        cost_estimate=pl.CostEstimate(flops=flops, transcendentals=0, bytes_accessed=1 << 20),
    )(parts, sums, ground_level_map)
    from_left = shift(right, "col", 1)
    from_right = shift(left, "col", -1)
    inside = tile_columns - half
    inner = pl.pallas_call(
        functools.partial(inner_kernel, first_slot),
        out_shape=jax.ShapeDtypeStruct((tile_rows, inside), F32),
        in_specs=[vmem()] * 4,
        out_specs=vmem(),
        scratch_shapes=[pltpu.VMEM((inside, 2 * tile_rows), F32)],
        compiler_params=params(),
        cost_estimate=pl.CostEstimate(flops=flops, transcendentals=0, bytes_accessed=1 << 20),
    )(parts, stack, mean, ground_level_map)

    wide = jax.ShapeDtypeStruct((tile_rows, tile_columns + LANES), F32)
    edge = jax.ShapeDtypeStruct((2 * SWEEPS, tile_columns + LANES), F32)
    height, land, top, bottom = pl.pallas_call(
        extend_kernel,
        out_shape=(wide, wide, edge, edge),
        in_specs=[vmem()] * 5,
        out_specs=(vmem(),) * 4,
        compiler_params=params(),
    )(outer, inner, ground_level_map, from_left, from_right)
    from_above = shift(bottom, "row", 1)
    from_below = shift(top, "row", -1)
    tile = jax.ShapeDtypeStruct((tile_rows, tile_columns), F32)
    depth = pl.pallas_call(
        functools.partial(middle_kernel, row_count, col_count),
        out_shape=tile,
        in_specs=[vmem()] * 2,
        out_specs=vmem(),
        compiler_params=params(),
        cost_estimate=pl.CostEstimate(
            flops=100 * tile_rows * tile_columns, transcendentals=0, bytes_accessed=1 << 22
        ),
    )(height, land)
    return pl.pallas_call(
        functools.partial(band_kernel, row_count, col_count),
        out_shape=tile,
        in_specs=[vmem()] * 5,
        out_specs=hbm,
        scratch_shapes=[pltpu.VMEM((2, 8, tile_columns), F32), pltpu.SemaphoreType.DMA((3,))],
        compiler_params=params(),
    )(height, land, from_above, from_below, depth)


def solution(mesh):
    in_specs = (
        P("row", "col"),
        P(("row", "col"), None),
        P(("row", "col")),
        P(("row", "col"), None, None),
        P(("row", "col"), None),
    )
    out_specs = P("row", "col")
    return jax.shard_map(body, mesh=mesh, in_specs=in_specs, out_specs=out_specs, check_vma=False)
```

```python
import functools

import jax
import jax.numpy as jnp
from jax import lax
from jax.experimental import pallas as pl
from jax.experimental.pallas import tpu as pltpu
from jax.sharding import PartitionSpec as P

SEGS = 4
SWEEPS = 4
MOST = 6
LANES = 128

spread = 4.0
tau_weight = 4.0
flow_gain = 8.0

F32 = jnp.float32
BF16 = jnp.bfloat16
VMEM_LIMIT = 24 * 1024 * 1024


def vmem():
    return pl.BlockSpec(memory_space=pltpu.VMEM)


def smem():
    return pl.BlockSpec(memory_space=pltpu.SMEM)


def params(limit=VMEM_LIMIT):
    return pltpu.CompilerParams(vmem_limit_bytes=limit)


def one_hot(cond):
    return jnp.where(cond, 1.0, 0.0).astype(BF16)


def pack_kernel(
    cover_hbm,
    ids_hbm,
    entry_hbm,
    place_hbm,
    ground_hbm,
    out_ref,
    ground_ref,
    cover_copy_ref,
    cover_ref,
    ids_ref,
    entry_ref,
    place_ref,
    used_ref,
    sems,
):
    owners, _, _ = out_ref.shape
    covers, bodies = cover_ref.shape
    copies = [
        pltpu.make_async_copy(source, target, sems.at[k])
        for k, (source, target) in enumerate(
            (
                (ids_hbm, ids_ref),
                (entry_hbm, entry_ref),
                (place_hbm, place_ref),
                (cover_hbm, cover_ref),
                (cover_hbm, cover_copy_ref),
                (ground_hbm, ground_ref),
            )
        )
    ]
    for copy in copies:
        copy.start()
    chunks = ids_ref.shape[0]
    sum_rows, count_rows = bodies * SEGS, bodies // 2
    first_slot = sum_rows + count_rows
    out_ref[:, first_slot:, :] = jnp.zeros((owners, MOST * 8, LANES), F32)
    for copy in copies:
        copy.wait()
    seg_iota = lax.broadcasted_iota(jnp.int32, (owners * sum_rows, LANES), 0)
    pair_iota = lax.broadcasted_iota(jnp.int32, (owners * count_rows, LANES), 0)
    lane_group = lax.broadcasted_iota(jnp.int32, (LANES, LANES), 0) // 16
    ids = [ids_ref[k : k + 1, :] for k in range(chunks)]
    by_pair = jnp.concatenate([one_hot(pair_iota == v // 8) for v in ids], axis=1)
    by_lane = jnp.concatenate([one_hot(lane_group == v % 8) for v in ids], axis=1)
    counts = lax.dot_general(
        by_pair, by_lane, (((1,), (1,)), ((), ())), preferred_element_type=F32
    )
    by_segment = jnp.concatenate([one_hot(seg_iota == v) for v in ids], axis=1)
    entries = entry_ref[...]
    high = entries.astype(BF16)
    low = (entries - high.astype(F32)).astype(BF16)
    both = jnp.dot(
        by_segment, jnp.concatenate([high, low], axis=1), preferred_element_type=F32
    )
    sums = both[:, :LANES] + both[:, LANES:]
    for owner in range(owners):
        out_ref[owner, :sum_rows, :] = sums[owner * sum_rows : (owner + 1) * sum_rows]
        out_ref[owner, sum_rows:first_slot, :] = counts[
            owner * count_rows : (owner + 1) * count_rows
        ]
    for column in range(owners):
        used_ref[column] = 0
    for body_id in range(bodies):
        rows = place_ref[body_id]
        tile = jnp.concatenate(
            [
                rows[axis : axis + 1, s * LANES : (s + 1) * LANES]
                for axis in range(2)
                for s in range(SEGS)
            ],
            axis=0,
        )
        for k in range(covers):
            column = cover_ref[k, body_id]
            slot = used_ref[column]
            used_ref[column] = slot + 1
            out_ref[column, pl.ds(pl.multiple_of(first_slot + slot * 8, 8), 8), :] = tile


def owner_kernel(cover_ref, part_ref, out_ref, total_ref, used_ref):
    columns = out_ref.shape[0]
    covers, bodies = cover_ref.shape
    rows = total_ref.shape[0]
    total = part_ref[0, :rows, :]
    for source in range(1, part_ref.shape[0]):
        total = total + part_ref[source, :rows, :]
    total_ref[...] = total
    out_ref[...] = jnp.zeros_like(out_ref)
    for column in range(columns):
        used_ref[column] = 0
    for body_id in range(bodies):
        sums = total_ref[body_id * SEGS : (body_id + 1) * SEGS, :]
        row, lane = bodies * SEGS + body_id // 2, 64 * (body_id % 2)
        count = total_ref[row : row + 1, lane : lane + 64]
        for k in range(covers):
            column = cover_ref[k, body_id]
            slot = used_ref[column]
            used_ref[column] = slot + 1
            out_ref[column, pl.ds(slot * SEGS, SEGS), :] = sums
            out_ref[column, pl.ds(MOST * SEGS + slot, 1), :64] = count
    for column in range(columns):
        out_ref[column, MOST * SEGS + MOST : MOST * SEGS + MOST + 1, :] = jnp.full(
            (1, LANES), used_ref[column].astype(F32), F32
        )


def lorentz(base, step):
    distance = base + step
    return 1.0 / (1.0 + distance * distance)


def cell_base(origin, coord):
    index = lax.broadcasted_iota(jnp.int32, (16, LANES), 0).astype(F32) * (1.0 / spread)
    return index - (coord - origin) * (1.0 / spread)


def column_block(place_ref, owner, row, origin, starts):
    parts = []
    for s in range(SEGS):
        base = cell_base(origin, place_ref[owner, row + SEGS + s : row + SEGS + s + 1, :])
        parts.append(
            jnp.concatenate(
                [
                    lorentz(base, (start + j) / spread).astype(BF16)
                    for start in starts
                    for j in range(0, LANES, 16)
                ],
                axis=0,
            )
        )
    return jnp.concatenate(parts, axis=1)


def times_stack(columns, stack):
    return lax.dot_general(
        columns, stack, (((1,), (1,)), ((), ())), preferred_element_type=F32
    )


def surface(acc, mean, ground):
    tile_rows = ground.shape[0]
    num = jnp.transpose(acc[:, :tile_rows])
    den = jnp.transpose(acc[:, tile_rows:])
    depth = (num + (mean - ground) * den) / (den + tau_weight)
    return jnp.maximum(depth, 0.0)


def for_used_slots(owners, codes, run):
    for group, code in enumerate(codes):

        @pl.loop(0, min(8, owners - 8 * group))
        def _(k):
            used = lax.shift_right_logical(code, 3 * k) & 7
            for slots in range(2, MOST + 1, 2):

                @pl.when((used <= slots) & (used > slots - 2))
                def _():
                    run(8 * group + k, slots)


def outer_kernel(
    first_slot, place_ref, sums_ref, ground_ref, depth_ref, left_ref, right_ref, stack_ref, mean_ref, acc_ref
):
    tile_rows, tile_columns = ground_ref.shape
    owners = sums_ref.shape[0]
    row_origin = (lax.axis_index("row") * tile_rows).astype(F32)
    col_origin = (lax.axis_index("col") * tile_columns).astype(F32)
    elev = jnp.sum(sums_ref[:, : MOST * SEGS, :], axis=0)
    count = jnp.sum(sums_ref[:, MOST * SEGS : MOST * SEGS + MOST, :], axis=0)
    elev = jnp.sum(jnp.sum(elev, axis=0, keepdims=True), axis=1, keepdims=True)
    count = jnp.sum(jnp.sum(count, axis=0, keepdims=True), axis=1, keepdims=True)
    mean = elev / jnp.maximum(count * (LANES / 16), 1.0)
    mean_ref[...] = jnp.broadcast_to(mean, mean_ref.shape)
    codes = []
    for group in range((owners + 7) // 8):
        code = jnp.zeros((1, 1), F32)
        for owner in range(8 * group, min(8 * group + 8, owners)):
            used = sums_ref[owner, MOST * SEGS + MOST : MOST * SEGS + MOST + 1, 0:1]
            code = code + used * (8.0 ** (owner % 8))
        mean_ref[group + 1 : group + 2, :] = jnp.broadcast_to(code, (1, LANES))
        codes.append(jnp.max(code).astype(jnp.int32))
    acc_ref[...] = jnp.zeros_like(acc_ref)
    starts = (0, tile_columns - LANES)

    def run(owner, slots):
        for slot in range(slots):
            row = first_slot + slot * 8
            blocks = []
            for s in range(SEGS):
                here = sums_ref[owner, MOST * SEGS + slot : MOST * SEGS + slot + 1, s * 16 : s * 16 + 1]
                part = sums_ref[owner, slot * SEGS + s : slot * SEGS + s + 1, :] - mean * here
                weight = jnp.broadcast_to(here, (16, LANES))
                part = jnp.broadcast_to(part, (16, LANES))
                base = cell_base(row_origin, place_ref[owner, row + s : row + s + 1, :])
                values = [lorentz(base, i / spread) for i in range(0, tile_rows, 16)]
                block = jnp.concatenate(
                    [(v * part).astype(BF16) for v in values]
                    + [(v * weight).astype(BF16) for v in values],
                    axis=0,
                )
                stack_ref[owner * (MOST * SEGS) + slot * SEGS + s] = block
                blocks.append(block)
            columns = column_block(place_ref, owner, row, col_origin, starts)
            acc_ref[...] += times_stack(columns, jnp.concatenate(blocks, axis=1))

    for_used_slots(owners, codes, run)
    ground = jnp.concatenate(
        [ground_ref[:, start : start + LANES] for start in starts], axis=1
    )
    depth = surface(acc_ref[...], mean, ground)
    depth_ref[...] = depth
    for out_ref, start, pick in ((left_ref, 0, 0), (right_ref, LANES, LANES - SWEEPS)):
        for k, values in enumerate((depth, ground)):
            out_ref[k * SWEEPS : (k + 1) * SWEEPS, :] = jnp.transpose(
                values[:, start : start + LANES]
            )[pick : pick + SWEEPS]


def inner_kernel(first_slot, place_ref, stack_ref, mean_ref, ground_ref, depth_ref, acc_ref):
    tile_columns = ground_ref.shape[1]
    owners = place_ref.shape[0]
    col_origin = (lax.axis_index("col") * tile_columns).astype(F32)
    acc_ref[...] = jnp.zeros_like(acc_ref)
    starts = tuple(range(LANES, tile_columns - LANES, LANES))
    codes = [
        jnp.max(mean_ref[group + 1 : group + 2, :]).astype(jnp.int32)
        for group in range((owners + 7) // 8)
    ]

    def run(owner, slots):
        for slot in range(slots):
            columns = column_block(place_ref, owner, first_slot + slot * 8, col_origin, starts)
            stack = jnp.concatenate(
                [stack_ref[owner * (MOST * SEGS) + slot * SEGS + s] for s in range(SEGS)], axis=1
            )
            acc_ref[...] += times_stack(columns, stack)

    for_used_slots(owners, codes, run)
    ground = ground_ref[:, LANES : tile_columns - LANES]
    depth_ref[...] = surface(acc_ref[...], mean_ref[0:1, 0:1], ground)


def extend_kernel(
    outer_ref, inner_ref, ground_ref, left_ref, right_ref, height_ref, land_ref, first_ref, second_ref
):
    tile_rows, tile_columns = ground_ref.shape
    sides = jnp.transpose(jnp.concatenate([left_ref[...], right_ref[...]], axis=0))
    blank = jnp.zeros((tile_rows, LANES - 2 * SWEEPS), F32)
    height_ref[:, :LANES] = outer_ref[:, :LANES]
    height_ref[:, LANES : tile_columns - LANES] = inner_ref[...]
    height_ref[:, tile_columns - LANES : tile_columns] = outer_ref[:, LANES:]
    land_ref[:, :tile_columns] = ground_ref[...]
    for k, ref in enumerate((height_ref, land_ref)):
        left = sides[:, k * SWEEPS : (k + 1) * SWEEPS]
        right = sides[:, (2 + k) * SWEEPS : (3 + k) * SWEEPS]
        ref[:, tile_columns:] = jnp.concatenate([right, blank, left], axis=1)
        rows = slice(k * SWEEPS, (k + 1) * SWEEPS)
        top, bottom = ref[:SWEEPS, :], ref[tile_rows - SWEEPS :, :]
        even = lax.rem(lax.axis_index("row"), 2) == 0
        first_ref[rows, :] = jnp.where(even, bottom, top)
        second_ref[rows, :] = jnp.where(even, top, bottom)


def relax(height, land, row_id, row_count, col_count, tile_rows, tile_columns):
    rows, cols = height.shape
    row_id = row_id + lax.axis_index("row") * tile_rows
    col_id = lax.broadcasted_iota(jnp.int32, (1, cols), 1)
    col_id = jnp.where(col_id < tile_columns + LANES // 2, col_id, col_id - cols)
    col_id = col_id + lax.axis_index("col") * tile_columns
    grid_rows, grid_cols = tile_rows * row_count, tile_columns * col_count
    gain_down = jnp.where((row_id >= 0) & (row_id < grid_rows - 1), flow_gain, 0.0)
    gain_right = jnp.where((col_id >= 0) & (col_id < grid_cols - 1), flow_gain, 0.0)
    down = gain_down / (1.0 + jnp.abs(land - pltpu.roll(land, rows - 1, 0)))
    right = gain_right / (1.0 + jnp.abs(land - pltpu.roll(land, cols - 1, 1)))
    up = pltpu.roll(down, 1, 0)
    left = pltpu.roll(right, 1, 1)
    scale = 1.0 / (1.0 + up + down + left + right)
    up, down, left, right = up * scale, down * scale, left * scale, right * scale
    for _ in range(SWEEPS):
        height = (
            height * scale
            + up * pltpu.roll(height, 1, 0)
            + down * pltpu.roll(height, rows - 1, 0)
            + left * pltpu.roll(height, 1, 1)
            + right * pltpu.roll(height, cols - 1, 1)
        )
    return height


def middle_kernel(row_count, col_count, height_ref, land_ref, out_ref):
    tile_rows, tile_columns = out_ref.shape
    row_id = lax.broadcasted_iota(jnp.int32, (tile_rows, 1), 0)
    height = relax(
        height_ref[...], land_ref[...], row_id, row_count, col_count, tile_rows, tile_columns
    )
    out_ref[...] = height[:, :tile_columns]


def band_kernel(
    row_count, col_count, height_ref, land_ref, first_ref, second_ref, middle_ref, out_hbm, rows_ref, sems
):
    tile_rows, tile_columns = out_hbm.shape
    keep = 16 - SWEEPS
    middle = pl.ds(8, tile_rows - 16)
    middle_copy = pltpu.make_async_copy(middle_ref.at[middle, :], out_hbm.at[middle, :], sems.at[2])
    middle_copy.start()

    def bands(ref, k):
        halo = slice(k * SWEEPS, (k + 1) * SWEEPS)
        even = lax.rem(lax.axis_index("row"), 2) == 0
        first, second = first_ref[halo, :], second_ref[halo, :]
        above, below = jnp.where(even, second, first), jnp.where(even, first, second)
        return jnp.concatenate(
            [above, ref[:keep, :], ref[tile_rows - keep :, :], below],
            axis=0,
        )

    row_id = lax.broadcasted_iota(jnp.int32, (32, 1), 0)
    row_id = jnp.where(row_id < 16, row_id - SWEEPS, row_id - 16 + tile_rows - keep)
    height = relax(
        bands(height_ref, 0), bands(land_ref, 1), row_id, row_count, col_count, tile_rows, tile_columns
    )
    rows_ref[0] = height[SWEEPS : SWEEPS + 8, :tile_columns]
    rows_ref[1] = height[16 + SWEEPS : 24 + SWEEPS, :tile_columns]
    copies = [
        pltpu.make_async_copy(rows_ref.at[k], out_hbm.at[pl.ds(first, 8), :], sems.at[k])
        for k, first in enumerate((0, tile_rows - 8))
    ]
    for copy in copies:
        copy.start()
    for copy in copies:
        copy.wait()
    middle_copy.wait()


def shift(values, axis, step):
    count = lax.axis_size(axis)
    return lax.ppermute(values, axis, [(i, (i + step) % count) for i in range(count)])


def body(
    ground_level_map,
    shoreline_altitude_entries,
    shoreline_piece_position,
    lake_panel_locations,
    spanned_patch_verticals,
):
    tile_rows, tile_columns = ground_level_map.shape
    col_count = lax.axis_size("col")
    row_count = lax.axis_size("row")
    records, _ = shoreline_altitude_entries.shape
    bodies, _ = spanned_patch_verticals.shape
    covers = spanned_patch_verticals.T
    first_slot = bodies * SEGS + bodies // 2
    hbm = pl.BlockSpec(memory_space=pltpu.HBM)

    parts, ground_level_map, covers = pl.pallas_call(
        pack_kernel,
        out_shape=(
            jax.ShapeDtypeStruct((col_count, first_slot + MOST * 8, LANES), F32),
            jax.ShapeDtypeStruct(ground_level_map.shape, F32),
            jax.ShapeDtypeStruct(covers.shape, jnp.int32),
        ),
        in_specs=[hbm] * 5,
        out_specs=(vmem(),) * 3,
        scratch_shapes=[
            pltpu.SMEM(covers.shape, jnp.int32),
            pltpu.VMEM((records // LANES, LANES), jnp.int32),
            pltpu.VMEM((records, LANES), F32),
            pltpu.VMEM(lake_panel_locations.shape, F32),
            pltpu.SMEM((col_count,), jnp.int32),
            pltpu.SemaphoreType.DMA((6,)),
        ],
        compiler_params=params(),
    )(
        *(
            pltpu.with_memory_space_constraint(value, pltpu.HBM)
            for value in (
                covers,
                shoreline_piece_position.reshape(records // LANES, LANES),
                shoreline_altitude_entries,
                lake_panel_locations,
                ground_level_map,
            )
        )
    )
    parts = lax.all_to_all(parts, "col", 0, 0, tiled=True)

    slot_rows = MOST * SEGS + 8
    sums = pl.pallas_call(
        owner_kernel,
        out_shape=jax.ShapeDtypeStruct((col_count, slot_rows, LANES), F32),
        in_specs=[smem(), vmem()],
        out_specs=vmem(),
        scratch_shapes=[
            pltpu.VMEM((first_slot, LANES), F32),
            pltpu.SMEM((col_count,), jnp.int32),
        ],
        compiler_params=params(),
    )(covers, parts)
    sums = lax.all_to_all(sums, "col", 0, 0, tiled=True)

    half = 2 * LANES
    blocks = col_count * MOST * SEGS
    flops = 4 * tile_rows * half * blocks * LANES
    edge = jax.ShapeDtypeStruct((2 * SWEEPS, tile_rows), F32)
    outer, left, right, stack, mean = pl.pallas_call(
        functools.partial(outer_kernel, first_slot),
        out_shape=(
            jax.ShapeDtypeStruct((tile_rows, half), F32),
            edge,
            edge,
            jax.ShapeDtypeStruct((blocks, 2 * tile_rows, LANES), BF16),
            jax.ShapeDtypeStruct((8, LANES), F32),
        ),
        in_specs=[vmem()] * 3,
        out_specs=(vmem(),) * 5,
        scratch_shapes=[pltpu.VMEM((half, 2 * tile_rows), F32)],
        compiler_params=params(),
        cost_estimate=pl.CostEstimate(flops=flops, transcendentals=0, bytes_accessed=1 << 20),
    )(parts, sums, ground_level_map)
    from_left = shift(right, "col", 1)
    from_right = shift(left, "col", -1)
    inside = tile_columns - half
    inner = pl.pallas_call(
        functools.partial(inner_kernel, first_slot),
        out_shape=jax.ShapeDtypeStruct((tile_rows, inside), F32),
        in_specs=[vmem()] * 4,
        out_specs=vmem(),
        scratch_shapes=[pltpu.VMEM((inside, 2 * tile_rows), F32)],
        compiler_params=params(),
        cost_estimate=pl.CostEstimate(flops=flops, transcendentals=0, bytes_accessed=1 << 20),
    )(parts, stack, mean, ground_level_map)

    wide = jax.ShapeDtypeStruct((tile_rows, tile_columns + LANES), F32)
    edge = jax.ShapeDtypeStruct((2 * SWEEPS, tile_columns + LANES), F32)
    height, land, first, second = pl.pallas_call(
        extend_kernel,
        out_shape=(wide, wide, edge, edge),
        in_specs=[vmem()] * 5,
        out_specs=(vmem(),) * 4,
        compiler_params=params(),
    )(outer, inner, ground_level_map, from_left, from_right)
    first = lax.ppermute(first, "row", [(i, i ^ 1) for i in range(row_count)])
    second = lax.ppermute(
        second, "row", [(i, (i + (1 if i % 2 else -1)) % row_count) for i in range(row_count)]
    )
    tile = jax.ShapeDtypeStruct((tile_rows, tile_columns), F32)
    depth = pl.pallas_call(
        functools.partial(middle_kernel, row_count, col_count),
        out_shape=tile,
        in_specs=[vmem()] * 2,
        out_specs=vmem(),
        compiler_params=params(),
        cost_estimate=pl.CostEstimate(
            flops=100 * tile_rows * tile_columns, transcendentals=0, bytes_accessed=1 << 22
        ),
    )(height, land)
    return pl.pallas_call(
        functools.partial(band_kernel, row_count, col_count),
        out_shape=tile,
        in_specs=[vmem()] * 5,
        out_specs=hbm,
        scratch_shapes=[pltpu.VMEM((2, 8, tile_columns), F32), pltpu.SemaphoreType.DMA((3,))],
        compiler_params=params(),
    )(height, land, first, second, depth)


def solution(mesh):
    in_specs = (
        P("row", "col"),
        P(("row", "col"), None),
        P(("row", "col")),
        P(("row", "col"), None, None),
        P(("row", "col"), None),
    )
    out_specs = P("row", "col")
    return jax.shard_map(body, mesh=mesh, in_specs=in_specs, out_specs=out_specs, check_vma=False)
```

```python
import functools

import jax
import jax.numpy as jnp
from jax import lax
from jax.experimental import pallas as pl
from jax.experimental.pallas import tpu as pltpu
from jax.sharding import PartitionSpec as P

SEGS = 4
SWEEPS = 4
MOST = 6
LANES = 128

spread = 4.0
tau_weight = 4.0
flow_gain = 8.0

F32 = jnp.float32
BF16 = jnp.bfloat16
VMEM_LIMIT = 24 * 1024 * 1024


def vmem():
    return pl.BlockSpec(memory_space=pltpu.VMEM)


def smem():
    return pl.BlockSpec(memory_space=pltpu.SMEM)


def params(limit=VMEM_LIMIT):
    return pltpu.CompilerParams(vmem_limit_bytes=limit)


def one_hot(cond):
    return jnp.where(cond, 1.0, 0.0).astype(BF16)


def pack_kernel(
    cover_hbm,
    ids_hbm,
    entry_hbm,
    place_hbm,
    ground_hbm,
    out_ref,
    ground_ref,
    cover_copy_ref,
    cover_ref,
    ids_ref,
    entry_ref,
    place_ref,
    used_ref,
    sems,
):
    owners, _, _ = out_ref.shape
    covers, bodies = cover_ref.shape
    copies = [
        pltpu.make_async_copy(source, target, sems.at[k])
        for k, (source, target) in enumerate(
            (
                (ids_hbm, ids_ref),
                (entry_hbm, entry_ref),
                (place_hbm, place_ref),
                (cover_hbm, cover_ref),
                (cover_hbm, cover_copy_ref),
                (ground_hbm, ground_ref),
            )
        )
    ]
    for copy in copies:
        copy.start()
    chunks = ids_ref.shape[0]
    sum_rows, count_rows = bodies * SEGS, bodies // 2
    first_slot = sum_rows + count_rows
    out_ref[:, first_slot:, :] = jnp.zeros((owners, MOST * 8, LANES), F32)
    for copy in copies:
        copy.wait()
    seg_iota = lax.broadcasted_iota(jnp.int32, (owners * sum_rows, LANES), 0)
    pair_iota = lax.broadcasted_iota(jnp.int32, (owners * count_rows, LANES), 0)
    lane_group = lax.broadcasted_iota(jnp.int32, (LANES, LANES), 0) // 16
    ids = [ids_ref[k : k + 1, :] for k in range(chunks)]
    by_pair = jnp.concatenate([one_hot(pair_iota == v // 8) for v in ids], axis=1)
    by_lane = jnp.concatenate([one_hot(lane_group == v % 8) for v in ids], axis=1)
    counts = lax.dot_general(
        by_pair, by_lane, (((1,), (1,)), ((), ())), preferred_element_type=F32
    )
    by_segment = jnp.concatenate([one_hot(seg_iota == v) for v in ids], axis=1)
    entries = entry_ref[...]
    high = entries.astype(BF16)
    low = (entries - high.astype(F32)).astype(BF16)
    both = jnp.dot(
        by_segment, jnp.concatenate([high, low], axis=1), preferred_element_type=F32
    )
    sums = both[:, :LANES] + both[:, LANES:]
    for owner in range(owners):
        out_ref[owner, :sum_rows, :] = sums[owner * sum_rows : (owner + 1) * sum_rows]
        out_ref[owner, sum_rows:first_slot, :] = counts[
            owner * count_rows : (owner + 1) * count_rows
        ]
    for column in range(owners):
        used_ref[column] = 0
    for body_id in range(bodies):
        rows = place_ref[body_id]
        tile = jnp.concatenate(
            [
                rows[axis : axis + 1, s * LANES : (s + 1) * LANES]
                for axis in range(2)
                for s in range(SEGS)
            ],
            axis=0,
        )
        for k in range(covers):
            column = cover_ref[k, body_id]
            slot = used_ref[column]
            used_ref[column] = slot + 1
            out_ref[column, pl.ds(pl.multiple_of(first_slot + slot * 8, 8), 8), :] = tile


def owner_kernel(cover_ref, part_ref, out_ref, total_ref, used_ref):
    columns = out_ref.shape[0]
    covers, bodies = cover_ref.shape
    rows = total_ref.shape[0]
    total = part_ref[0, :rows, :]
    for source in range(1, part_ref.shape[0]):
        total = total + part_ref[source, :rows, :]
    total_ref[...] = total
    out_ref[...] = jnp.zeros_like(out_ref)
    for column in range(columns):
        used_ref[column] = 0
    for body_id in range(bodies):
        sums = total_ref[body_id * SEGS : (body_id + 1) * SEGS, :]
        row, lane = bodies * SEGS + body_id // 2, 64 * (body_id % 2)
        count = total_ref[row : row + 1, lane : lane + 64]
        for k in range(covers):
            column = cover_ref[k, body_id]
            slot = used_ref[column]
            used_ref[column] = slot + 1
            out_ref[column, pl.ds(slot * SEGS, SEGS), :] = sums
            out_ref[column, pl.ds(MOST * SEGS + slot, 1), :64] = count
    for column in range(columns):
        out_ref[column, MOST * SEGS + MOST : MOST * SEGS + MOST + 1, :] = jnp.full(
            (1, LANES), used_ref[column].astype(F32), F32
        )


def lorentz(base, step):
    distance = base + step
    return 1.0 / (1.0 + distance * distance)


def cell_base(origin, coord):
    index = lax.broadcasted_iota(jnp.int32, (16, LANES), 0).astype(F32) * (1.0 / spread)
    return index - (coord - origin) * (1.0 / spread)


def column_block(place_ref, owner, row, origin, starts):
    parts = []
    for s in range(SEGS):
        base = cell_base(origin, place_ref[owner, row + SEGS + s : row + SEGS + s + 1, :])
        parts.append(
            jnp.concatenate(
                [
                    lorentz(base, (start + j) / spread).astype(BF16)
                    for start in starts
                    for j in range(0, LANES, 16)
                ],
                axis=0,
            )
        )
    return jnp.concatenate(parts, axis=1)


def times_stack(columns, stack):
    return lax.dot_general(
        columns, stack, (((1,), (1,)), ((), ())), preferred_element_type=F32
    )


def surface(acc, mean, ground):
    tile_rows = ground.shape[0]
    num = jnp.transpose(acc[:, :tile_rows])
    den = jnp.transpose(acc[:, tile_rows:])
    depth = (num + (mean - ground) * den) / (den + tau_weight)
    return jnp.maximum(depth, 0.0)


def for_used_slots(owners, codes, run):
    for group, code in enumerate(codes):

        @pl.loop(0, min(8, owners - 8 * group))
        def _(k):
            used = lax.shift_right_logical(code, 3 * k) & 7
            for slots in range(2, MOST + 1, 2):

                @pl.when((used <= slots) & (used > slots - 2))
                def _():
                    run(8 * group + k, slots)


def outer_kernel(
    first_slot, place_ref, sums_ref, ground_ref, depth_ref, first_ref, second_ref, stack_ref, mean_ref, acc_ref
):
    tile_rows, tile_columns = ground_ref.shape
    owners = sums_ref.shape[0]
    row_origin = (lax.axis_index("row") * tile_rows).astype(F32)
    col_origin = (lax.axis_index("col") * tile_columns).astype(F32)
    elev = jnp.sum(sums_ref[:, : MOST * SEGS, :], axis=0)
    count = jnp.sum(sums_ref[:, MOST * SEGS : MOST * SEGS + MOST, :], axis=0)
    elev = jnp.sum(jnp.sum(elev, axis=0, keepdims=True), axis=1, keepdims=True)
    count = jnp.sum(jnp.sum(count, axis=0, keepdims=True), axis=1, keepdims=True)
    mean = elev / jnp.maximum(count * (LANES / 16), 1.0)
    mean_ref[...] = jnp.broadcast_to(mean, mean_ref.shape)
    codes = []
    for group in range((owners + 7) // 8):
        code = jnp.zeros((1, 1), F32)
        for owner in range(8 * group, min(8 * group + 8, owners)):
            used = sums_ref[owner, MOST * SEGS + MOST : MOST * SEGS + MOST + 1, 0:1]
            code = code + used * (8.0 ** (owner % 8))
        mean_ref[group + 1 : group + 2, :] = jnp.broadcast_to(code, (1, LANES))
        codes.append(jnp.max(code).astype(jnp.int32))
    acc_ref[...] = jnp.zeros_like(acc_ref)
    starts = (0, tile_columns - LANES)

    def run(owner, slots):
        for slot in range(slots):
            row = first_slot + slot * 8
            blocks = []
            for s in range(SEGS):
                here = sums_ref[owner, MOST * SEGS + slot : MOST * SEGS + slot + 1, s * 16 : s * 16 + 1]
                part = sums_ref[owner, slot * SEGS + s : slot * SEGS + s + 1, :] - mean * here
                weight = jnp.broadcast_to(here, (16, LANES))
                part = jnp.broadcast_to(part, (16, LANES))
                base = cell_base(row_origin, place_ref[owner, row + s : row + s + 1, :])
                values = [lorentz(base, i / spread) for i in range(0, tile_rows, 16)]
                block = jnp.concatenate(
                    [(v * part).astype(BF16) for v in values]
                    + [(v * weight).astype(BF16) for v in values],
                    axis=0,
                )
                stack_ref[owner * (MOST * SEGS) + slot * SEGS + s] = block
                blocks.append(block)
            columns = column_block(place_ref, owner, row, col_origin, starts)
            acc_ref[...] += times_stack(columns, jnp.concatenate(blocks, axis=1))

    for_used_slots(owners, codes, run)
    ground = jnp.concatenate(
        [ground_ref[:, start : start + LANES] for start in starts], axis=1
    )
    depth = surface(acc_ref[...], mean, ground)
    depth_ref[...] = depth
    even = lax.rem(lax.axis_index("col"), 2) == 0
    for k, values in enumerate((depth, ground)):
        rows = slice(k * SWEEPS, (k + 1) * SWEEPS)
        left = jnp.transpose(values[:, :LANES])[:SWEEPS]
        right = jnp.transpose(values[:, LANES:])[LANES - SWEEPS :]
        first_ref[rows, :] = jnp.where(even, right, left)
        second_ref[rows, :] = jnp.where(even, left, right)


def inner_kernel(first_slot, place_ref, stack_ref, mean_ref, ground_ref, depth_ref, acc_ref):
    tile_columns = ground_ref.shape[1]
    owners = place_ref.shape[0]
    col_origin = (lax.axis_index("col") * tile_columns).astype(F32)
    acc_ref[...] = jnp.zeros_like(acc_ref)
    starts = tuple(range(LANES, tile_columns - LANES, LANES))
    codes = [
        jnp.max(mean_ref[group + 1 : group + 2, :]).astype(jnp.int32)
        for group in range((owners + 7) // 8)
    ]

    def run(owner, slots):
        for slot in range(slots):
            columns = column_block(place_ref, owner, first_slot + slot * 8, col_origin, starts)
            stack = jnp.concatenate(
                [stack_ref[owner * (MOST * SEGS) + slot * SEGS + s] for s in range(SEGS)], axis=1
            )
            acc_ref[...] += times_stack(columns, stack)

    for_used_slots(owners, codes, run)
    ground = ground_ref[:, LANES : tile_columns - LANES]
    depth_ref[...] = surface(acc_ref[...], mean_ref[0:1, 0:1], ground)


def extend_kernel(
    outer_ref, inner_ref, ground_ref, near_ref, far_ref, height_ref, land_ref, first_ref, second_ref
):
    tile_rows, tile_columns = ground_ref.shape
    even = lax.rem(lax.axis_index("col"), 2) == 0
    near, far = near_ref[...], far_ref[...]
    sides = jnp.concatenate([jnp.where(even, far, near), jnp.where(even, near, far)], axis=0)
    sides = jnp.transpose(sides)
    blank = jnp.zeros((tile_rows, LANES - 2 * SWEEPS), F32)
    height_ref[:, :LANES] = outer_ref[:, :LANES]
    height_ref[:, LANES : tile_columns - LANES] = inner_ref[...]
    height_ref[:, tile_columns - LANES : tile_columns] = outer_ref[:, LANES:]
    land_ref[:, :tile_columns] = ground_ref[...]
    for k, ref in enumerate((height_ref, land_ref)):
        left = sides[:, k * SWEEPS : (k + 1) * SWEEPS]
        right = sides[:, (2 + k) * SWEEPS : (3 + k) * SWEEPS]
        ref[:, tile_columns:] = jnp.concatenate([right, blank, left], axis=1)
        rows = slice(k * SWEEPS, (k + 1) * SWEEPS)
        top, bottom = ref[:SWEEPS, :], ref[tile_rows - SWEEPS :, :]
        even = lax.rem(lax.axis_index("row"), 2) == 0
        first_ref[rows, :] = jnp.where(even, bottom, top)
        second_ref[rows, :] = jnp.where(even, top, bottom)


def relax(height, land, row_id, row_count, col_count, tile_rows, tile_columns):
    rows, cols = height.shape
    row_id = row_id + lax.axis_index("row") * tile_rows
    col_id = lax.broadcasted_iota(jnp.int32, (1, cols), 1)
    col_id = jnp.where(col_id < tile_columns + LANES // 2, col_id, col_id - cols)
    col_id = col_id + lax.axis_index("col") * tile_columns
    grid_rows, grid_cols = tile_rows * row_count, tile_columns * col_count
    gain_down = jnp.where((row_id >= 0) & (row_id < grid_rows - 1), flow_gain, 0.0)
    gain_right = jnp.where((col_id >= 0) & (col_id < grid_cols - 1), flow_gain, 0.0)
    down = gain_down / (1.0 + jnp.abs(land - pltpu.roll(land, rows - 1, 0)))
    right = gain_right / (1.0 + jnp.abs(land - pltpu.roll(land, cols - 1, 1)))
    up = pltpu.roll(down, 1, 0)
    left = pltpu.roll(right, 1, 1)
    scale = 1.0 / (1.0 + up + down + left + right)
    up, down, left, right = up * scale, down * scale, left * scale, right * scale
    for _ in range(SWEEPS):
        height = (
            height * scale
            + up * pltpu.roll(height, 1, 0)
            + down * pltpu.roll(height, rows - 1, 0)
            + left * pltpu.roll(height, 1, 1)
            + right * pltpu.roll(height, cols - 1, 1)
        )
    return height


def middle_kernel(row_count, col_count, height_ref, land_ref, out_ref):
    tile_rows, tile_columns = out_ref.shape
    row_id = lax.broadcasted_iota(jnp.int32, (tile_rows, 1), 0)
    height = relax(
        height_ref[...], land_ref[...], row_id, row_count, col_count, tile_rows, tile_columns
    )
    out_ref[...] = height[:, :tile_columns]


def band_kernel(
    row_count, col_count, height_ref, land_ref, first_ref, second_ref, middle_ref, out_hbm, rows_ref, sems
):
    tile_rows, tile_columns = out_hbm.shape
    keep = 16 - SWEEPS
    middle = pl.ds(8, tile_rows - 16)
    middle_copy = pltpu.make_async_copy(middle_ref.at[middle, :], out_hbm.at[middle, :], sems.at[2])
    middle_copy.start()

    def bands(ref, k):
        halo = slice(k * SWEEPS, (k + 1) * SWEEPS)
        even = lax.rem(lax.axis_index("row"), 2) == 0
        first, second = first_ref[halo, :], second_ref[halo, :]
        above, below = jnp.where(even, second, first), jnp.where(even, first, second)
        return jnp.concatenate(
            [above, ref[:keep, :], ref[tile_rows - keep :, :], below],
            axis=0,
        )

    row_id = lax.broadcasted_iota(jnp.int32, (32, 1), 0)
    row_id = jnp.where(row_id < 16, row_id - SWEEPS, row_id - 16 + tile_rows - keep)
    height = relax(
        bands(height_ref, 0), bands(land_ref, 1), row_id, row_count, col_count, tile_rows, tile_columns
    )
    rows_ref[0] = height[SWEEPS : SWEEPS + 8, :tile_columns]
    rows_ref[1] = height[16 + SWEEPS : 24 + SWEEPS, :tile_columns]
    copies = [
        pltpu.make_async_copy(rows_ref.at[k], out_hbm.at[pl.ds(first, 8), :], sems.at[k])
        for k, first in enumerate((0, tile_rows - 8))
    ]
    for copy in copies:
        copy.start()
    for copy in copies:
        copy.wait()
    middle_copy.wait()


def swap(values, axis, odd):
    count = lax.axis_size(axis)
    pairs = [(i, (i + (1 if i % 2 == odd else -1)) % count) for i in range(count)]
    return lax.ppermute(values, axis, pairs)


def body(
    ground_level_map,
    shoreline_altitude_entries,
    shoreline_piece_position,
    lake_panel_locations,
    spanned_patch_verticals,
):
    tile_rows, tile_columns = ground_level_map.shape
    col_count = lax.axis_size("col")
    row_count = lax.axis_size("row")
    records, _ = shoreline_altitude_entries.shape
    bodies, _ = spanned_patch_verticals.shape
    covers = spanned_patch_verticals.T
    first_slot = bodies * SEGS + bodies // 2
    hbm = pl.BlockSpec(memory_space=pltpu.HBM)

    parts, ground_level_map, covers = pl.pallas_call(
        pack_kernel,
        out_shape=(
            jax.ShapeDtypeStruct((col_count, first_slot + MOST * 8, LANES), F32),
            jax.ShapeDtypeStruct(ground_level_map.shape, F32),
            jax.ShapeDtypeStruct(covers.shape, jnp.int32),
        ),
        in_specs=[hbm] * 5,
        out_specs=(vmem(),) * 3,
        scratch_shapes=[
            pltpu.SMEM(covers.shape, jnp.int32),
            pltpu.VMEM((records // LANES, LANES), jnp.int32),
            pltpu.VMEM((records, LANES), F32),
            pltpu.VMEM(lake_panel_locations.shape, F32),
            pltpu.SMEM((col_count,), jnp.int32),
            pltpu.SemaphoreType.DMA((6,)),
        ],
        compiler_params=params(),
    )(
        *(
            pltpu.with_memory_space_constraint(value, pltpu.HBM)
            for value in (
                covers,
                shoreline_piece_position.reshape(records // LANES, LANES),
                shoreline_altitude_entries,
                lake_panel_locations,
                ground_level_map,
            )
        )
    )
    parts = lax.all_to_all(parts, "col", 0, 0, tiled=True)

    slot_rows = MOST * SEGS + 8
    sums = pl.pallas_call(
        owner_kernel,
        out_shape=jax.ShapeDtypeStruct((col_count, slot_rows, LANES), F32),
        in_specs=[smem(), vmem()],
        out_specs=vmem(),
        scratch_shapes=[
            pltpu.VMEM((first_slot, LANES), F32),
            pltpu.SMEM((col_count,), jnp.int32),
        ],
        compiler_params=params(),
    )(covers, parts)
    sums = lax.all_to_all(sums, "col", 0, 0, tiled=True)

    half = 2 * LANES
    blocks = col_count * MOST * SEGS
    flops = 4 * tile_rows * half * blocks * LANES
    edge = jax.ShapeDtypeStruct((2 * SWEEPS, tile_rows), F32)
    outer, near, far, stack, mean = pl.pallas_call(
        functools.partial(outer_kernel, first_slot),
        out_shape=(
            jax.ShapeDtypeStruct((tile_rows, half), F32),
            edge,
            edge,
            jax.ShapeDtypeStruct((blocks, 2 * tile_rows, LANES), BF16),
            jax.ShapeDtypeStruct((8, LANES), F32),
        ),
        in_specs=[vmem()] * 3,
        out_specs=(vmem(),) * 5,
        scratch_shapes=[pltpu.VMEM((half, 2 * tile_rows), F32)],
        compiler_params=params(),
        cost_estimate=pl.CostEstimate(flops=flops, transcendentals=0, bytes_accessed=1 << 20),
    )(parts, sums, ground_level_map)
    near, far = swap(near, "col", 0), swap(far, "col", 1)
    inside = tile_columns - half
    inner = pl.pallas_call(
        functools.partial(inner_kernel, first_slot),
        out_shape=jax.ShapeDtypeStruct((tile_rows, inside), F32),
        in_specs=[vmem()] * 4,
        out_specs=vmem(),
        scratch_shapes=[pltpu.VMEM((inside, 2 * tile_rows), F32)],
        compiler_params=params(),
        cost_estimate=pl.CostEstimate(flops=flops, transcendentals=0, bytes_accessed=1 << 20),
    )(parts, stack, mean, ground_level_map)

    wide = jax.ShapeDtypeStruct((tile_rows, tile_columns + LANES), F32)
    edge = jax.ShapeDtypeStruct((2 * SWEEPS, tile_columns + LANES), F32)
    height, land, first, second = pl.pallas_call(
        extend_kernel,
        out_shape=(wide, wide, edge, edge),
        in_specs=[vmem()] * 5,
        out_specs=(vmem(),) * 4,
        compiler_params=params(),
    )(outer, inner, ground_level_map, near, far)
    first, second = swap(first, "row", 0), swap(second, "row", 1)
    tile = jax.ShapeDtypeStruct((tile_rows, tile_columns), F32)
    depth = pl.pallas_call(
        functools.partial(middle_kernel, row_count, col_count),
        out_shape=tile,
        in_specs=[vmem()] * 2,
        out_specs=vmem(),
        compiler_params=params(),
        cost_estimate=pl.CostEstimate(
            flops=100 * tile_rows * tile_columns, transcendentals=0, bytes_accessed=1 << 22
        ),
    )(height, land)
    return pl.pallas_call(
        functools.partial(band_kernel, row_count, col_count),
        out_shape=tile,
        in_specs=[vmem()] * 5,
        out_specs=hbm,
        scratch_shapes=[pltpu.VMEM((2, 8, tile_columns), F32), pltpu.SemaphoreType.DMA((3,))],
        compiler_params=params(),
    )(height, land, first, second, depth)


def solution(mesh):
    in_specs = (
        P("row", "col"),
        P(("row", "col"), None),
        P(("row", "col")),
        P(("row", "col"), None, None),
        P(("row", "col"), None),
    )
    out_specs = P("row", "col")
    return jax.shard_map(body, mesh=mesh, in_specs=in_specs, out_specs=out_specs, check_vma=False)
```
